256 devices in a mesh: section: 2 (over z_lo), fsdp: 32 (over z_hi, y, core), tensor: 4 (over x).
Axes of the slice: x: 4, y: 4, z: 8 (z_hi: 4, z_lo: 2; z = z_hi * 2 + z_lo), core: 2. Of those that a mesh axis runs over, the one named last changes fastest.
Arguments:
- frames: bfloat16 [4096, 3072], P('fsdp', 'tensor')
- lengths: int32 [32], P('fsdp'), may hold values from 16 to 128, as said below
- qkv_weight: bfloat16 [2, 3, 3072, 1536], P('section', None, 'fsdp', 'tensor'), as said below
- out_weight: bfloat16 [2, 1536, 3072], P('section', 'tensor', 'fsdp'), may hold values from -0.15625 to 0.15625
- grad_out: bfloat16 [4096, 3072], P('fsdp', 'tensor'), may hold values from -6 to 6
Outputs:
- input_grads: bfloat16 [2, 4096, 3072], P('section', 'fsdp', 'tensor')
- qkv_grad: bfloat16 [2, 3, 3072, 1536], P('section', None, 'fsdp', 'tensor')
- out_grad: bfloat16 [2, 1536, 3072], P('section', 'tensor', 'fsdp')
The draws below stay inside these ranges and needn't reach their ends.
Inputs may be any that keep to these rules, and one draw needn't show every extreme that they name: Utterance b's live frames are its first lengths[b] slots; some utterance fills all 128 slots. `qkv_weight`: index 0, 1, 2 of the second dimension are the query, key and value projections.
All inputs are finite; a program needn't handle non-finite values.
Results may differ from the reference program's by a relative error of at most 0.03.
Values may be sent and summed in bfloat16 or wider, within the bound.
No kernel may reach another device: no remote copies, remote signals or barrier semaphores. Data moves between devices by JAX's collectives and lax.ppermute only.
A program may use at most 64 MiB of HBM per device.

```python
import jax
import jax.numpy as jnp
from jax import lax

D = 3072
HEADS = 12
HEAD = 128
LMAX = 128
UTTS = 32
FRAMES = 4096
N_FSDP = 32


def draw_frames(key, part):
    normal_part = jax.random.normal(key, (FRAMES, D), jnp.float32)
    return normal_part.astype(jnp.bfloat16)


def draw_lengths(key, part):
    drawn = jax.random.randint(key, (UTTS,), LMAX // 8, LMAX + 1, jnp.int32)
    chosen = jax.random.randint(jax.random.fold_in(key, 3), (), 0, UTTS, jnp.int32)
    return jnp.where(jnp.arange(UTTS, dtype=jnp.int32) == chosen, LMAX, drawn).astype(jnp.int32)


def draw_qkv_weight(key, part):
    width_all = HEADS * HEAD
    draws_base = jax.random.normal(key, (2, 3, D, width_all), jnp.float32) * float(D) ** (-0.5)
    return draws_base.astype(jnp.bfloat16)


def block_levels(rng, extent, shards, low, high):
    factor_of = 1.0
    for axis_at, parts in shards:
        draws = jax.random.uniform(jax.random.fold_in(jax.random.fold_in(rng, 6), axis_at), (parts,), jnp.float32, low / len(shards), high / len(shards))
        factor_of = factor_of * jnp.repeat(jnp.exp(draws), extent[axis_at] // parts).reshape((-1,) + (1,) * (len(extent) - 1 - axis_at))
    return factor_of


def normal_values(own_key, shape, width, reach, pieces=(), held_as=jnp.bfloat16):
    result = jax.random.normal(own_key, shape, jnp.float32) * width
    if len(pieces) > 0:
        result = block_levels(own_key, shape, pieces, -0.22, 0.18) * result
    return jnp.clip(result, min=-reach, max=reach).astype(held_as)


def setup_inputs(seed: int = 0) -> dict:
    key_list = jax.random.split(jax.random.key(seed), 6)
    frames = draw_frames(jax.random.fold_in(key_list[5], 71), 0)
    lengths = draw_lengths(jax.random.fold_in(key_list[5], 71), 0)
    qkv_weight = draw_qkv_weight(jax.random.fold_in(key_list[5], 71), 0)
    out_weight = normal_values(key_list[3], (2, HEADS * HEAD, D), (HEADS * HEAD) ** -0.5, 0.15625, ((0, 2), (1, 4), (2, 32)))
    grad_out = normal_values(key_list[4], (FRAMES, D), 1.0, 6.0, ((0, 32), (1, 4)))
    return {"frames": frames, "lengths": lengths, "qkv_weight": qkv_weight, "out_weight": out_weight, "grad_out": grad_out}


EPSILON = 1e-05

def norm_rows(hidden_in):
    widened = hidden_in.astype(jnp.float32)
    average = lax.optimization_barrier(jnp.mean(widened, axis=-1, keepdims=True))
    centered = widened - average
    variance = lax.optimization_barrier(jnp.mean(centered * centered, axis=-1, keepdims=True))
    inverse = lax.rsqrt(variance + EPSILON)
    return (centered * inverse, inverse)

def attend_forward(queries, key_rows, values, live_keys):
    score_scale = float(HEAD) ** (-0.5)
    scores = jnp.einsum('bqhe,bkhe->bhqk', queries.astype(jnp.float32), key_rows.astype(jnp.float32)) * score_scale
    scores = jnp.where(live_keys[:, None, None, :], scores, jnp.float32(-1e+30))
    highest = lax.optimization_barrier(jnp.max(scores, axis=-1, keepdims=True))
    raised = jnp.exp(scores - highest)
    attend = raised / lax.optimization_barrier(jnp.sum(raised, axis=-1, keepdims=True))
    attend_low = attend.astype(jnp.bfloat16)
    context = jnp.einsum('bhqk,bkhe->bqhe', attend_low.astype(jnp.float32), values.astype(jnp.float32)).astype(jnp.bfloat16)
    return (attend, attend_low, context)

def attend_backward(grad_context, queries, key_rows, values, attend, attend_low):
    score_scale = float(HEAD) ** (-0.5)
    grad_attend = jnp.einsum('bqhe,bkhe->bhqk', grad_context.astype(jnp.float32), values.astype(jnp.float32))
    grad_values = jnp.einsum('bhqk,bqhe->bkhe', attend_low.astype(jnp.float32), grad_context.astype(jnp.float32)).astype(jnp.bfloat16)
    inner = lax.optimization_barrier(jnp.sum(grad_attend * attend, axis=-1, keepdims=True))
    grad_scores = (attend * (grad_attend - inner) * score_scale).astype(jnp.bfloat16)
    grad_queries = jnp.einsum('bhqk,bkhe->bqhe', grad_scores.astype(jnp.float32), key_rows.astype(jnp.float32)).astype(jnp.bfloat16)
    grad_keys = jnp.einsum('bhqk,bqhe->bkhe', grad_scores.astype(jnp.float32), queries.astype(jnp.float32)).astype(jnp.bfloat16)
    return (grad_queries, grad_keys, grad_values)

def layer_forward(hidden_in, w_qkv, w_out, live_keys, live_rows):
    unit_rows, inverse = norm_rows(hidden_in)
    normed = unit_rows.astype(jnp.bfloat16)
    projected = jnp.einsum('rd,cdh->crh', normed.astype(jnp.float32), w_qkv.astype(jnp.float32)).astype(jnp.bfloat16)
    utterances, length = live_keys.shape
    split_qkv = projected.reshape(3, utterances, length, -1, HEAD)
    attend, attend_low, context = attend_forward(split_qkv[0], split_qkv[1], split_qkv[2], live_keys)
    context = context.reshape(utterances * length, -1)
    mixed = jnp.dot(context, w_out, preferred_element_type=jnp.float32)
    output = (hidden_in.astype(jnp.float32) + live_rows * mixed).astype(jnp.bfloat16)
    return (output, (unit_rows, inverse, normed, split_qkv, attend, attend_low, context))

def layer_backward(grad_top, kept_state, w_qkv, w_out, live_rows):
    unit_rows, inverse, normed, split_qkv, attend, attend_low, context = kept_state
    masked = (live_rows * grad_top.astype(jnp.float32)).astype(jnp.bfloat16)
    grad_context = jnp.dot(masked, w_out.T, preferred_element_type=jnp.float32).astype(jnp.bfloat16)
    grad_context = grad_context.reshape(split_qkv.shape[1:])
    grad_queries, grad_keys, grad_values = attend_backward(grad_context, split_qkv[0], split_qkv[1], split_qkv[2], attend, attend_low)
    frame_rows = grad_top.shape[0]
    grad_qkv = jnp.stack([grad_queries, grad_keys, grad_values]).reshape(3, frame_rows, -1)
    norm_grad = jnp.einsum('crh,cdh->rd', grad_qkv.astype(jnp.float32), w_qkv.astype(jnp.float32))
    centered = norm_grad - lax.optimization_barrier(jnp.mean(norm_grad, axis=-1, keepdims=True)) - unit_rows * lax.optimization_barrier(jnp.mean(norm_grad * unit_rows, axis=-1, keepdims=True))
    grad_in = (grad_top.astype(jnp.float32) + inverse * centered).astype(jnp.bfloat16)
    return (grad_in, masked, grad_qkv, normed, context)

def weight_grads(normed, masked, grad_qkv, context):
    group_rows = FRAMES // N_FSDP
    full_width = normed.shape[1]
    head_width = context.shape[1]

    def one_group(totals, index):
        first_row = (index * group_rows).astype(jnp.int32)
        normed_part = lax.dynamic_slice_in_dim(normed, first_row, group_rows, 0)
        masked_part = lax.dynamic_slice_in_dim(masked, first_row, group_rows, 0)
        context_part = lax.dynamic_slice_in_dim(context, first_row, group_rows, 0)
        grad_part = lax.dynamic_slice_in_dim(grad_qkv, first_row, group_rows, 1)
        term_qkv = jnp.einsum('rd,crh->cdh', normed_part.astype(jnp.float32), grad_part.astype(jnp.float32))
        term_out = jnp.dot(context_part.T, masked_part, preferred_element_type=jnp.float32)
        rounded = lax.optimization_barrier((term_qkv.astype(jnp.bfloat16), term_out.astype(jnp.bfloat16)))
        return ((totals[0] + rounded[0].astype(jnp.float32), totals[1] + rounded[1].astype(jnp.float32)), None)
    start_sums = (jnp.zeros((3, full_width, head_width), jnp.float32), jnp.zeros((head_width, full_width), jnp.float32))
    totals, _ = lax.scan(one_group, start_sums, jnp.arange(N_FSDP, dtype=jnp.int32))
    return (totals[0].astype(jnp.bfloat16), totals[1].astype(jnp.bfloat16))

def reference(frames, lengths, qkv_weight, out_weight, grad_out):
    live_keys = jnp.arange(LMAX, dtype=jnp.int32)[None, :] < lengths[:, None]
    live_rows = live_keys.reshape(FRAMES, 1).astype(jnp.float32)
    first_out, state_first = layer_forward(frames, qkv_weight[0], out_weight[0], live_keys, live_rows)
    second_out, state_second = layer_forward(first_out, qkv_weight[1], out_weight[1], live_keys, live_rows)
    grad_upper, masked_upper, qkv_upper, normed_upper, context_upper = layer_backward(grad_out, state_second, qkv_weight[1], out_weight[1], live_rows)
    grad_lower, masked_lower, qkv_lower, normed_lower, context_lower = layer_backward(grad_upper, state_first, qkv_weight[0], out_weight[0], live_rows)
    lower_qkv, lower_out = weight_grads(normed_lower, masked_lower, qkv_lower, context_lower)
    upper_qkv, upper_out = weight_grads(normed_upper, masked_upper, qkv_upper, context_upper)
    input_grads = jnp.stack([grad_lower, grad_upper])
    return (input_grads, jnp.stack([lower_qkv, upper_qkv]), jnp.stack([lower_out, upper_out]))
```

```python
import jax
import jax.numpy as jnp
from jax import lax
from jax.experimental import pallas as pl
from jax.experimental.pallas import tpu as pltpu
from jax.sharding import PartitionSpec as P

HEAD = 128
EPSILON = 1e-05
F32 = jnp.float32
BF16 = jnp.bfloat16
VMEM_LIMIT = 56 << 20

REL_GET = (0, 3, 1, 2)
REL_PUT = (0, 1, 3, 2)


def shift_tensor(value, step):
    count = lax.axis_size("tensor")
    return lax.ppermute(value, "tensor", [(i, (i + step) % count) for i in range(count)])


def cross_section(value, source):
    return lax.ppermute(value, "section", [(source, 1 - source)])


def shift_grid(value, phase, step):
    pairs = []
    for section in range(2):
        along_z = (section == 0) == (phase == 0)
        for z in range(4):
            for y in range(4):
                for core in range(2):
                    to_z, to_y = ((z + step) % 4, y) if along_z else (z, (y + step) % 4)
                    pairs.append(
                        (section * 32 + z * 8 + y * 2 + core, section * 32 + to_z * 8 + to_y * 2 + core)
                    )
    return lax.ppermute(value, ("section", "fsdp"), pairs)


def swap_cores(value):
    count = lax.axis_size("fsdp")
    return lax.ppermute(value, "fsdp", [(i, i ^ 1) for i in range(count)])


def gather_tensor(own):
    return (own, shift_tensor(own, 1), shift_tensor(own, -1), shift_tensor(own, 2))


def gather_weights(shard):
    behind, ahead = shift_grid(shard, 0, 1), shift_grid(shard, 0, -1)
    low, high = shift_grid(behind[:2], 0, 1), shift_grid(ahead[2:], 0, -1)
    line = jnp.stack([shard, behind, ahead, jnp.concatenate([low, high], 0)])
    behind, ahead = shift_grid(line, 1, 1), shift_grid(line, 1, -1)
    low, high = shift_grid(behind[:2], 1, 1), shift_grid(ahead[2:], 1, -1)
    mine = (line, behind, ahead, low, high)
    return mine, tuple(swap_cores(part) for part in mine)


def add(*terms):
    total = terms[0].astype(F32)
    for term in terms[1:]:
        total = total + term.astype(F32)
    return total.astype(BF16)


def reduce_line(blocks, phase):
    own, ahead, behind, opposite = blocks
    low, high = shift_grid(opposite[:2], phase, 1), shift_grid(opposite[2:], phase, -1)
    ahead = jnp.concatenate([add(ahead[:2], low), ahead[2:]], 0)
    behind = jnp.concatenate([behind[:2], add(behind[2:], high)], 0)
    return add(own, shift_grid(ahead, phase, 1), shift_grid(behind, phase, -1))


def reduce_weights(mine, other):
    summed = [add(a, swap_cores(b)) for a, b in zip(mine, other)]
    line = reduce_line(summed, 1)
    return reduce_line([line[0], line[1], line[2], line[3]], 0)


def dot_nn(a, b):
    return jnp.dot(a, b, preferred_element_type=F32)


def dot_nt(a, b):
    return lax.dot_general(a, b, (((1,), (1,)), ((), ())), preferred_element_type=F32)


def dot_tn(a, b):
    return lax.dot_general(a, b, (((0,), (0,)), ((), ())), preferred_element_type=F32)


def block_of(info, rel):
    return lax.rem(info[0] + rel, 4)


def rows_of(ref, block, width):
    return ref[pl.ds(pl.multiple_of(block * width, width), width), :]


def live_column(info, rows):
    return lax.broadcasted_iota(jnp.int32, (rows, 1), 0) < info[5]


def row_moments(x_refs):
    width = sum(ref.shape[1] for ref in x_refs)
    total = sum(jnp.sum(ref[...].astype(F32), axis=-1, keepdims=True) for ref in x_refs)
    mean = total / width
    square = 0.0
    for ref in x_refs:
        centered = ref[...].astype(F32) - mean
        square = square + jnp.sum(centered * centered, axis=-1, keepdims=True)
    return mean, lax.rsqrt(square / width + EPSILON)


def project(info, x_refs, w_ref, mean, inverse, normed_ref=None):
    totals = [None, None, None]
    for rel, ref in zip(REL_GET, x_refs):
        block = block_of(info, rel)
        normed = ((ref[...].astype(F32) - mean) * inverse).astype(BF16)
        if normed_ref is not None:
            normed_ref[block] = normed
        for c in range(3):
            part = dot_nn(normed, rows_of(w_ref.at[c], block, ref.shape[1]))
            totals[c] = part if totals[c] is None else totals[c] + part
    return [total.astype(BF16) for total in totals]


def attend_head(info, queries, keys, values):
    rows = queries.shape[0]
    scores = dot_nt(queries, keys) * (float(HEAD) ** -0.5)
    live_keys = lax.broadcasted_iota(jnp.int32, (rows, rows), 1) < info[5]
    scores = jnp.where(live_keys, scores, F32(-1e30))
    raised = jnp.exp(scores - jnp.max(scores, axis=-1, keepdims=True))
    attend = raised / jnp.sum(raised, axis=-1, keepdims=True)
    return attend, dot_nn(attend.astype(BF16), values).astype(BF16)


def head_slices(width):
    return [slice(start, start + HEAD) for start in range(0, width, HEAD)]


def first_kernel(info, *refs):
    x_refs, parts = refs[:4], refs[4:14]
    wq_ref, wo_ref = refs[14:16]
    mixed_refs = refs[16:20]
    context_ref, sems = refs[20:]
    section = info[4]
    rows = parts[0].shape[2]
    copies = []
    for side in range(2):
        arrays = parts[side * 5 : side * 5 + 5]
        core = info[3] if side == 0 else 1 - info[3]
        for far, rel_far in enumerate(REL_GET):
            for near, rel_near in enumerate(REL_GET):
                if far < 3:
                    source = arrays[far].at[near]
                else:
                    source = arrays[3 + near // 2].at[near % 2]
                rel_z = lax.select(section == 0, rel_near, rel_far)
                rel_y = lax.select(section == 0, rel_far, rel_near)
                z, y = lax.rem(info[1] + rel_z, 4), lax.rem(info[2] + rel_y, 4)
                start = pl.multiple_of(((z * 4 + y) * 2 + core) * rows, rows)
                number = len(copies)
                copies.append(
                    pltpu.make_async_copy(
                        source.at[pl.ds(0, 3)], wq_ref.at[:, pl.ds(start, rows), :], sems.at[number]
                    )
                )
                copies.append(
                    pltpu.make_async_copy(
                        source.at[3], wo_ref.at[pl.ds(start, rows), :], sems.at[number + 1]
                    )
                )
    for copy in copies:
        copy.start()
    mean, inverse = row_moments(x_refs)
    for copy in copies:
        copy.wait()
    queries, keys, values = project(info, x_refs, wq_ref, mean, inverse)
    for cols in head_slices(queries.shape[1]):
        _, context_ref[:, cols] = attend_head(info, queries[:, cols], keys[:, cols], values[:, cols])
    context = context_ref[...]
    for rel, ref in zip(REL_PUT, mixed_refs):
        ref[...] = dot_nt(context, rows_of(wo_ref, block_of(info, rel), ref.shape[1])).astype(ref.dtype)


def forward_kernel(info, *refs):
    x_refs, w_ref = refs[:4], refs[4]
    normed_ref, qkv_ref, attend_ref, context_ref, moment_ref = refs[5:]
    mean, inverse = row_moments(x_refs)
    moment_ref[:, 0:1] = mean
    moment_ref[:, 1:2] = inverse
    queries, keys, values = project(info, x_refs, w_ref, mean, inverse, normed_ref)
    qkv_ref[0] = queries
    qkv_ref[1] = keys
    qkv_ref[2] = values
    for head, cols in enumerate(head_slices(queries.shape[1])):
        attend, context = attend_head(info, queries[:, cols], keys[:, cols], values[:, cols])
        attend_ref[head] = attend
        context_ref[:, cols] = context


def context_grad_kernel(info, *refs):
    g_refs, w_ref = refs[:4], refs[4]
    grad_ref, masked_ref = refs[5:]
    live = live_column(info, g_refs[0].shape[0])
    total = None
    for rel, ref in zip(REL_GET, g_refs):
        block = block_of(info, rel)
        masked = jnp.where(live, ref[...].astype(F32), 0.0).astype(BF16)
        masked_ref[block] = masked
        part = dot_nn(masked, rows_of(w_ref, block, ref.shape[1]))
        total = part if total is None else total + part
    grad_ref[...] = total.astype(BF16)


def backward_kernel(info, *refs):
    x_refs = refs[:4]
    moment_ref, qkv_ref, attend_ref, grad_ref, w_ref = refs[4:9]
    gq_ref, stat_ref = refs[9:11]
    norm_refs = refs[11:15]
    scale = float(HEAD) ** -0.5
    for head, cols in enumerate(head_slices(grad_ref.shape[1])):
        grad = grad_ref[:, cols]
        queries, keys, values = (qkv_ref[c, :, cols] for c in range(3))
        attend = attend_ref[head]
        grad_attend = dot_nt(grad, values)
        gq_ref[2, :, cols] = dot_tn(attend.astype(BF16), grad).astype(BF16)
        inner = jnp.sum(grad_attend * attend, axis=-1, keepdims=True)
        grad_scores = (attend * (grad_attend - inner) * scale).astype(BF16)
        gq_ref[0, :, cols] = dot_nn(grad_scores, keys).astype(BF16)
        gq_ref[1, :, cols] = dot_tn(grad_scores, queries).astype(BF16)
    mean, inverse = moment_ref[:, 0:1], moment_ref[:, 1:2]
    width = x_refs[0].shape[1]
    plain, weighted = 0.0, 0.0
    by_rel = dict(zip(REL_GET, x_refs))
    for rel, ref in zip(REL_PUT, norm_refs):
        block = block_of(info, rel)
        part = None
        for c in range(3):
            term = dot_nt(gq_ref[c], rows_of(w_ref.at[c], block, width))
            part = term if part is None else part + term
        unit = (by_rel[rel][...].astype(F32) - mean) * inverse
        plain = plain + jnp.sum(part, axis=-1, keepdims=True)
        weighted = weighted + jnp.sum(part * unit, axis=-1, keepdims=True)
        ref[:, :width] = part.astype(ref.dtype)
    stat_ref[:, 0:1] = plain
    stat_ref[:, 1:2] = weighted
    lane = lax.broadcasted_iota(jnp.int32, (plain.shape[0], 128), 1)
    plain_high, weighted_high = plain.astype(BF16).astype(F32), weighted.astype(BF16).astype(F32)
    packed = jnp.where(lane == 0, plain_high, jnp.where(lane == 1, plain - plain_high, 0.0))
    packed = jnp.where(lane == 2, weighted_high, jnp.where(lane == 3, weighted - weighted_high, packed))
    for ref in norm_refs[1:]:
        ref[:, width:] = packed.astype(BF16)


def weight_grad_kernel(info, *refs):
    normed_ref, masked_ref, gq_ref, context_ref = refs[:4]
    outs = refs[4:12]
    block_ref = refs[12]
    section = info[4]
    rows = outs[0].shape[2]
    for z in range(4):
        for c in range(4):
            left = normed_ref[z] if c < 3 else masked_ref[z]
            right = gq_ref[c] if c < 3 else context_ref[...]
            block_ref[c, z] = dot_tn(left, right).astype(BF16)
    for far, rel_far in enumerate(REL_PUT):
        for near, rel_near in enumerate(REL_PUT):
            rel_z = lax.select(section == 0, rel_near, rel_far)
            rel_y = lax.select(section == 0, rel_far, rel_near)
            z, y = lax.rem(info[1] + rel_z, 4), lax.rem(info[2] + rel_y, 4)
            for side in range(2):
                core = info[3] if side == 0 else 1 - info[3]
                start = pl.multiple_of((y * 2 + core) * rows, rows)
                for c in range(4):
                    outs[side * 4 + far][near, c] = block_ref[c, z, pl.ds(start, rows), :]


VMEM = pl.BlockSpec(memory_space=pltpu.VMEM)
SMEM = pl.BlockSpec(memory_space=pltpu.SMEM)
ANY = pl.BlockSpec(memory_space=pl.ANY)


def call(kernel, out_types, in_specs, scratch, flops, args):
    moved = sum(a.size * a.dtype.itemsize for a in args)
    return pl.pallas_call(
        kernel,
        out_shape=out_types,
        in_specs=in_specs,
        out_specs=jax.tree.map(lambda _: VMEM, out_types),
        scratch_shapes=scratch,
        compiler_params=pltpu.CompilerParams(vmem_limit_bytes=VMEM_LIMIT),
        cost_estimate=pl.CostEstimate(flops=flops, bytes_accessed=moved, transcendentals=0),
    )(*args)


def shape(dims, dtype=BF16):
    return jax.ShapeDtypeStruct(dims, dtype)


def local(frames, lengths, qkv_weight, out_weight, grad_out):
    rows, own_width = frames.shape
    heads_width = qkv_weight.shape[3]
    heads = heads_width // HEAD
    width = own_width * lax.axis_size("tensor")
    place = lax.axis_index("fsdp")
    section = lax.axis_index("section")
    on_first = section == 0
    info = jnp.stack(
        [
            lax.axis_index("tensor"),
            place // 8,
            place // 2 % 4,
            place % 2,
            section,
            lengths[0],
        ]
    ).astype(jnp.int32)
    live_rows = (jnp.arange(rows, dtype=jnp.int32)[:, None] < lengths[0]).astype(F32)

    shard = jnp.concatenate([qkv_weight[0], out_weight[0].T[None]], 0)
    mine, other = gather_weights(shard)
    x_first = gather_tensor(frames)
    g_first = gather_tensor(grad_out)

    block = (rows, own_width)
    wide = (rows, own_width + 128)
    project_flops = 2 * rows * width * 3 * heads_width
    w_qkv, w_out, *mixed = call(
        first_kernel,
        [
            shape((3, width, heads_width)),
            shape((width, heads_width)),
            shape(block, F32),
            shape(block),
            shape(block),
            shape(block),
        ],
        [SMEM] + [VMEM] * 4 + [ANY] * 10,
        [pltpu.VMEM((rows, heads_width), BF16), pltpu.SemaphoreType.DMA((64,))],
        project_flops,
        (info, *x_first, *mine, *other),
    )

    def context_grad(pieces):
        return call(
            context_grad_kernel,
            [shape((rows, heads_width)), shape((4, *block))],
            [SMEM] + [VMEM] * 5,
            [],
            project_flops // 3,
            (info, *pieces, w_out),
        )

    def backward(x_pieces, moments, qkv, attend, grad_context, own_grad):
        gq, stats, *parts = call(
            backward_kernel,
            [
                shape((3, rows, heads_width)),
                shape((rows, 2), F32),
                shape(block, F32),
                shape(wide),
                shape(wide),
                shape(wide),
            ],
            [SMEM] + [VMEM] * 9,
            [],
            project_flops,
            (info, *x_pieces, moments, qkv, attend, grad_context, w_qkv),
        )
        arrived = [shift_tensor(part, step) for part, step in zip(parts[1:], (1, -1, 2))]
        norm_grad = parts[0]
        plain, weighted = stats[:, 0:1], stats[:, 1:2]
        for part in arrived:
            part = part.astype(F32)
            norm_grad = norm_grad + part[:, :own_width]
            plain = plain + (part[:, own_width : own_width + 1] + part[:, own_width + 1 : own_width + 2])
            weighted = weighted + (
                part[:, own_width + 2 : own_width + 3] + part[:, own_width + 3 : own_width + 4]
            )
        mean, inverse = moments[:, 0:1], moments[:, 1:2]
        unit = (x_pieces[0].astype(F32) - mean) * inverse
        centered = norm_grad - plain / width - unit * (weighted / width)
        return gq, (own_grad.astype(F32) + inverse * centered).astype(BF16)

    arrived = [shift_tensor(part, step) for part, step in zip(mixed[1:], (1, -1, 2))]
    mixed_own = mixed[0] + sum(part.astype(F32) for part in arrived)
    first_out = (frames.astype(F32) + live_rows * mixed_own).astype(BF16)
    grad_context_top, _ = context_grad(g_first)

    entry = jnp.where(on_first, frames, cross_section(first_out, 0))
    x_entry = gather_tensor(entry)
    normed, qkv, attend, context, moments = call(
        forward_kernel,
        [
            shape((4, *block)),
            shape((3, rows, heads_width)),
            shape((heads, rows, rows), F32),
            shape((rows, heads_width)),
            shape((rows, 2), F32),
        ],
        [SMEM] + [VMEM] * 5,
        [],
        project_flops,
        (info, *x_entry, w_qkv),
    )
    _, upper_grad = backward(x_entry, moments, qkv, attend, grad_context_top, grad_out)
    top_grad = jnp.where(on_first, cross_section(upper_grad, 1), grad_out)
    grad_context, masked = context_grad(gather_tensor(top_grad))
    gq, grad_in = backward(x_entry, moments, qkv, attend, grad_context, top_grad)

    part = shape((4, 4, width // 32, heads_width))
    blocks = call(
        weight_grad_kernel,
        [part] * 8,
        [SMEM] + [VMEM] * 4,
        [pltpu.VMEM((4, 4, own_width, heads_width), BF16)],
        4 * project_flops // 3,
        (info, normed, masked, gq, context),
    )
    summed = reduce_weights(blocks[:4], blocks[4:])
    return (grad_in[None], summed[None, :3], summed[3].T[None])


def solution(mesh):
    in_specs = (
        P("fsdp", "tensor"),
        P("fsdp"),
        P("section", None, "fsdp", "tensor"),
        P("section", "tensor", "fsdp"),
        P("fsdp", "tensor"),
    )
    out_specs = (
        P("section", "fsdp", "tensor"),
        P("section", None, "fsdp", "tensor"),
        P("section", "tensor", "fsdp"),
    )
    return jax.shard_map(local, mesh=mesh, in_specs=in_specs, out_specs=out_specs, check_vma=False)
```

```python
import jax
import jax.numpy as jnp
from jax import lax
from jax.experimental import pallas as pl
from jax.experimental.pallas import tpu as pltpu
from jax.sharding import PartitionSpec as P

HEAD = 128
EPSILON = 1e-05
F32 = jnp.float32
BF16 = jnp.bfloat16
VMEM_LIMIT = 56 << 20

REL_GET = (0, 3, 1, 2)
REL_PUT = (0, 1, 3, 2)


def shift_tensor(value, step):
    count = lax.axis_size("tensor")
    return lax.ppermute(value, "tensor", [(i, (i + step) % count) for i in range(count)])


def cross_section(value, source):
    return lax.ppermute(value, "section", [(source, 1 - source)])


def shift_grid(value, axis, step):
    pairs = []
    for z in range(4):
        for y in range(4):
            for core in range(2):
                to_z, to_y = ((z + step) % 4, y) if axis == "z" else (z, (y + step) % 4)
                pairs.append((z * 8 + y * 2 + core, to_z * 8 + to_y * 2 + core))
    return lax.ppermute(value, "fsdp", pairs)


def swap_cores(value):
    count = lax.axis_size("fsdp")
    return lax.ppermute(value, "fsdp", [(i, i ^ 1) for i in range(count)])


def gather_tensor(own):
    opposite = shift_tensor(own, 2)
    return (own, shift_tensor(own, 1), shift_tensor(own, -1), opposite)


def ring_get(value, axis):
    half = value.shape[0] // 2
    behind, ahead = shift_grid(value, axis, 1), shift_grid(value, axis, -1)
    return behind, ahead, shift_grid(behind[:half], axis, 1), shift_grid(ahead[half:], axis, -1)


def gather_weights(shard, near_axis, far_axis):
    behind, ahead, low, high = ring_get(shard, near_axis)
    line = jnp.stack([shard, behind, ahead, jnp.concatenate([low, high], 0)])
    mine = (line, *ring_get(line, far_axis))
    return mine + tuple(swap_cores(part) for part in mine)


def add(*terms):
    total = terms[0].astype(F32)
    for term in terms[1:]:
        total = total + term.astype(F32)
    return total.astype(BF16)


def ring_put(blocks, axis):
    own, ahead, behind, opposite = blocks
    half = own.shape[0] // 2
    low, high = shift_grid(opposite[:half], axis, 1), shift_grid(opposite[half:], axis, -1)
    ahead = jnp.concatenate([add(ahead[:half], low), ahead[half:]], 0)
    behind = jnp.concatenate([behind[:half], add(behind[half:], high)], 0)
    return add(own, shift_grid(ahead, axis, 1), shift_grid(behind, axis, -1))


def reduce_weights(mine, other, near_axis, far_axis):
    summed = [add(a, swap_cores(b)) for a, b in zip(mine, other)]
    line = ring_put(summed, far_axis)
    return ring_put([line[0], line[1], line[2], line[3]], near_axis)


def dot_nn(a, b):
    return jnp.dot(a, b, preferred_element_type=F32)


def dot_nt(a, b):
    return lax.dot_general(a, b, (((1,), (1,)), ((), ())), preferred_element_type=F32)


def dot_tn(a, b):
    return lax.dot_general(a, b, (((0,), (0,)), ((), ())), preferred_element_type=F32)


def block_of(info, rel):
    return lax.rem(info[0] + rel, 4)


def rows_of(ref, block, width):
    return ref[pl.ds(pl.multiple_of(block * width, width), width), :]


def live_column(info, rows):
    return lax.broadcasted_iota(jnp.int32, (rows, 1), 0) < info[5]


def row_moments(x_refs):
    width = sum(ref.shape[1] for ref in x_refs)
    total = sum(jnp.sum(ref[...].astype(F32), axis=-1, keepdims=True) for ref in x_refs)
    mean = total / width
    square = 0.0
    for ref in x_refs:
        centered = ref[...].astype(F32) - mean
        square = square + jnp.sum(centered * centered, axis=-1, keepdims=True)
    return mean, lax.rsqrt(square / width + EPSILON)


def project(info, x_refs, w_ref, mean, inverse, normed_ref=None, copies=None):
    totals = [None, None, None]
    for index, (rel, ref) in enumerate(zip(REL_GET, x_refs)):
        block = block_of(info, rel)
        normed = ((ref[...].astype(F32) - mean) * inverse).astype(BF16)
        if normed_ref is not None:
            normed_ref[block] = normed
        if copies is not None:
            copies[index].wait()
        for c in range(3):
            part = dot_nn(normed, rows_of(w_ref.at[c], block, ref.shape[1]))
            totals[c] = part if totals[c] is None else totals[c] + part
    return [total.astype(BF16) for total in totals]


def attend_head(info, queries, keys, values):
    rows = queries.shape[0]
    scores = dot_nt(queries, keys) * (float(HEAD) ** -0.5)
    live_keys = lax.broadcasted_iota(jnp.int32, (rows, rows), 1) < info[5]
    scores = jnp.where(live_keys, scores, F32(-1e30))
    raised = jnp.exp(scores - jnp.max(scores, axis=-1, keepdims=True))
    attend = raised / jnp.sum(raised, axis=-1, keepdims=True)
    return attend, dot_nn(attend.astype(BF16), values).astype(BF16)


def head_slices(width):
    return [slice(start, start + HEAD) for start in range(0, width, HEAD)]


def place_row(info, rel_z, rel_y, core, rows):
    z, y = lax.rem(info[1] + rel_z, 4), lax.rem(info[2] + rel_y, 4)
    return pl.multiple_of(((z * 4 + y) * 2 + core) * rows, rows)


def part_copies(info, parts, along_z_first, make):
    rows = 2 * parts[0].shape[-2]
    for side in range(2):
        arrays = parts[side * 5 : side * 5 + 5]
        core = info[3] if side == 0 else 1 - info[3]
        for far, rel_far in enumerate(REL_GET):
            for near, rel_near in enumerate(REL_GET):
                if far < 3:
                    source = arrays[far].at[near]
                else:
                    source = arrays[3 + near // 2].at[near % 2]
                rel_z, rel_y = (rel_near, rel_far) if along_z_first else (rel_far, rel_near)
                start = place_row(info, rel_z, rel_y, core, rows)
                for half in range(2):
                    make(source.at[half], pl.multiple_of(start + half * (rows // 2), rows // 2))


def first_kernel(info, *refs):
    x_refs, q_parts, o_parts = refs[:4], refs[4:14], refs[14:24]
    wq_out, wo_out = refs[24:26]
    mixed_refs = refs[26:30]
    wq_ref, wo_ref, context_ref, q_sems, o_sems, out_sems = refs[30:]
    q_copies, o_copies = [], []
    half = q_parts[0].shape[-2]

    def make_q(source, row):
        target = wq_ref.at[:, pl.ds(row, half), :]
        q_copies.append(pltpu.make_async_copy(source, target, q_sems.at[len(q_copies)]))

    def make_o(source, row):
        target = wo_ref.at[pl.ds(row, half), :]
        o_copies.append(pltpu.make_async_copy(source, target, o_sems.at[len(o_copies)]))

    part_copies(info, q_parts, True, make_q)
    part_copies(info, o_parts, False, make_o)
    for copy in q_copies + o_copies:
        copy.start()
    mean, inverse = row_moments(x_refs)
    for copy in q_copies:
        copy.wait()
    save_q = pltpu.make_async_copy(wq_ref, wq_out, out_sems.at[0])
    save_q.start()
    queries, keys, values = project(info, x_refs, wq_ref, mean, inverse)
    for copy in o_copies:
        copy.wait()
    save_o = pltpu.make_async_copy(wo_ref, wo_out, out_sems.at[1])
    save_o.start()
    for cols in head_slices(queries.shape[1]):
        _, context_ref[:, cols] = attend_head(info, queries[:, cols], keys[:, cols], values[:, cols])
    context = context_ref[...]
    for rel, ref in zip(REL_PUT, mixed_refs):
        ref[...] = dot_nt(context, rows_of(wo_ref, block_of(info, rel), ref.shape[1])).astype(ref.dtype)
    save_q.wait()
    save_o.wait()


def load_blocks(info, order, w_hbm, w_ref, sems):
    width = w_ref.shape[-2] // 4
    copies = []
    for rel in order:
        rows = pl.ds(pl.multiple_of(block_of(info, rel) * width, width), width)
        where = (slice(None), rows) if len(w_ref.shape) == 3 else (rows,)
        copies.append(pltpu.make_async_copy(w_hbm.at[where], w_ref.at[where], sems.at[len(copies)]))
    for copy in copies:
        copy.start()
    return copies


def context_grad(info, g_refs, w_ref, masked_ref=None, copies=None):
    live = live_column(info, g_refs[0].shape[0])
    total = None
    for index, (rel, ref) in enumerate(zip(REL_GET, g_refs)):
        block = block_of(info, rel)
        masked = jnp.where(live, ref[...].astype(F32), 0.0).astype(BF16)
        if masked_ref is not None:
            masked_ref[block] = masked
        if copies is not None:
            copies[index].wait()
        part = dot_nn(masked, rows_of(w_ref, block, ref.shape[1]))
        total = part if total is None else total + part
    return total.astype(BF16)


def context_grad_kernel(info, *refs):
    g_refs, w_hbm, grad_ref, w_ref, sems = refs[:4], refs[4], refs[5], refs[6], refs[7]
    copies = load_blocks(info, REL_GET, w_hbm, w_ref, sems)
    grad_ref[...] = context_grad(info, g_refs, w_ref, copies=copies)


def attend_backward(qkv_ref, attend_ref, grad, gq_ref):
    scale = float(HEAD) ** -0.5
    for head, cols in enumerate(head_slices(grad.shape[1])):
        grad_head = grad[:, cols]
        queries, keys, values = (qkv_ref[c, :, cols] for c in range(3))
        attend = attend_ref[head]
        grad_attend = dot_nt(grad_head, values)
        gq_ref[2, :, cols] = dot_tn(attend.astype(BF16), grad_head).astype(BF16)
        inner = jnp.sum(grad_attend * attend, axis=-1, keepdims=True)
        grad_scores = (attend * (grad_attend - inner) * scale).astype(BF16)
        gq_ref[0, :, cols] = dot_nn(grad_scores, keys).astype(BF16)
        gq_ref[1, :, cols] = dot_tn(grad_scores, queries).astype(BF16)


def norm_parts(info, x_refs, mean, inverse, gq_ref, w_ref, stat_ref, norm_refs, order, copies=None):
    width = x_refs[0].shape[1]
    plain, weighted = 0.0, 0.0
    by_rel = dict(zip(REL_GET, x_refs))
    out_by_rel = dict(zip(REL_PUT, norm_refs))
    for index, rel in enumerate(order):
        block = block_of(info, rel)
        if copies is not None:
            copies[index].wait()
        part = None
        for c in range(3):
            term = dot_nt(gq_ref[c], rows_of(w_ref.at[c], block, width))
            part = term if part is None else part + term
        unit = (by_rel[rel][...].astype(F32) - mean) * inverse
        plain = plain + jnp.sum(part, axis=-1, keepdims=True)
        weighted = weighted + jnp.sum(part * unit, axis=-1, keepdims=True)
        ref = out_by_rel[rel]
        ref[:, :width] = part.astype(ref.dtype)
    stat_ref[:, 0:1] = plain
    stat_ref[:, 1:2] = weighted
    lane = lax.broadcasted_iota(jnp.int32, (plain.shape[0], 128), 1)
    plain_high, weighted_high = plain.astype(BF16).astype(F32), weighted.astype(BF16).astype(F32)
    packed = jnp.where(lane == 0, plain_high, jnp.where(lane == 1, plain - plain_high, 0.0))
    packed = jnp.where(lane == 2, weighted_high, jnp.where(lane == 3, weighted - weighted_high, packed))
    for ref in norm_refs[1:]:
        ref[:, width:] = packed.astype(BF16)


def middle_kernel(info, *refs):
    x_refs, grad_ref, w_hbm = refs[:4], refs[4], refs[5]
    normed_ref, qkv_ref, attend_ref, context_ref, moment_ref, stat_ref = refs[6:12]
    norm_refs, gq_ref, w_ref, sems = refs[12:16], refs[16], refs[17], refs[18]
    copies = load_blocks(info, REL_GET, w_hbm, w_ref, sems)
    mean, inverse = row_moments(x_refs)
    moment_ref[:, 0:1] = mean
    moment_ref[:, 1:2] = inverse
    queries, keys, values = project(info, x_refs, w_ref, mean, inverse, normed_ref, copies)
    qkv_ref[0] = queries
    qkv_ref[1] = keys
    qkv_ref[2] = values
    for head, cols in enumerate(head_slices(queries.shape[1])):
        attend, context = attend_head(info, queries[:, cols], keys[:, cols], values[:, cols])
        attend_ref[head] = attend
        context_ref[:, cols] = context
    attend_backward(qkv_ref, attend_ref, grad_ref[...], gq_ref)
    norm_parts(info, x_refs, mean, inverse, gq_ref, w_ref, stat_ref, norm_refs, REL_PUT)


def norm_kernel(info, *refs):
    x_refs, moment_ref, gq_ref, w_hbm = refs[:4], refs[4], refs[5], refs[6]
    stat_ref, norm_refs, w_ref, sems = refs[7], refs[8:12], refs[12], refs[13]
    order = (2, 1, 3, 0)
    copies = load_blocks(info, order, w_hbm, w_ref, sems)
    mean, inverse = moment_ref[:, 0:1], moment_ref[:, 1:2]
    norm_parts(info, x_refs, mean, inverse, gq_ref, w_ref, stat_ref, norm_refs, order, copies)


def last_kernel(info, *refs):
    g_refs, w_hbm, qkv_ref, attend_ref, normed_ref, context_ref = refs[:4], *refs[4:9]
    gq_ref, q_outs, o_outs = refs[9], refs[10:18], refs[18:26]
    w_ref, masked_ref, block_ref, sems = refs[26:30]
    copies = load_blocks(info, REL_GET, w_hbm, w_ref, sems)
    grad = context_grad(info, g_refs, w_ref, masked_ref, copies)
    attend_backward(qkv_ref, attend_ref, grad, gq_ref)
    half = q_outs[0].shape[-2]
    for c in range(4):
        for z in range(4):
            left = normed_ref[z] if c < 3 else masked_ref[z]
            right = gq_ref[c] if c < 3 else context_ref[...]
            block_ref[c, pl.ds(z * left.shape[1], left.shape[1]), :] = dot_tn(left, right).astype(BF16)
    for side in range(2):
        core = info[3] if side == 0 else 1 - info[3]
        for far, rel_far in enumerate(REL_PUT):
            for near, rel_near in enumerate(REL_PUT):
                q_start = place_row(info, rel_near, rel_far, core, 2 * half)
                o_start = place_row(info, rel_far, rel_near, core, 2 * half)
                for part in range(2):
                    q_rows = pl.ds(pl.multiple_of(q_start + part * half, half), half)
                    o_rows = pl.ds(pl.multiple_of(o_start + part * half, half), half)
                    for c in range(3):
                        q_outs[side * 4 + far][near, part, c] = block_ref[c, q_rows, :]
                    o_outs[side * 4 + far][near, part] = block_ref[3, o_rows, :]


VMEM = pl.BlockSpec(memory_space=pltpu.VMEM)
SMEM = pl.BlockSpec(memory_space=pltpu.SMEM)
ANY = pl.BlockSpec(memory_space=pl.ANY)


def call(kernel, outs, in_specs, scratch, flops, args, out_specs=None):
    moved = sum(a.size * a.dtype.itemsize for a in args)
    return pl.pallas_call(
        kernel,
        out_shape=outs,
        in_specs=in_specs,
        out_specs=out_specs or [VMEM] * len(outs),
        scratch_shapes=scratch,
        compiler_params=pltpu.CompilerParams(vmem_limit_bytes=VMEM_LIMIT),
        cost_estimate=pl.CostEstimate(flops=flops, bytes_accessed=moved, transcendentals=0),
    )(*args)


def shape(dims, dtype=BF16):
    return jax.ShapeDtypeStruct(dims, dtype)


def local(frames, lengths, qkv_weight, out_weight, grad_out):
    rows, own_width = frames.shape
    shard_rows, heads_width = qkv_weight.shape[2:]
    heads = heads_width // HEAD
    width = own_width * lax.axis_size("tensor")
    place = lax.axis_index("fsdp")
    on_first = lax.axis_index("section") == 0
    info = jnp.stack(
        [lax.axis_index("tensor"), place // 8, place // 2 % 4, place % 2, 0, lengths[0]]
    ).astype(jnp.int32)
    live_rows = (jnp.arange(rows, dtype=jnp.int32)[:, None] < lengths[0]).astype(F32)

    half = shard_rows // 2
    q_shard = qkv_weight[0].reshape(3, 2, half, heads_width).transpose(1, 0, 2, 3)
    o_shard = out_weight[0].T.reshape(2, half, heads_width)
    q_parts = gather_weights(q_shard, "z", "y")
    o_parts = gather_weights(o_shard, "y", "z")
    x_first, g_first = lax.optimization_barrier((gather_tensor(frames), gather_tensor(grad_out)))

    block = (rows, own_width)
    wide = (rows, own_width + 128)
    wq_dims, wo_dims = (3, width, heads_width), (width, heads_width)
    project_flops = 2 * rows * width * 3 * heads_width
    block_sems = pltpu.SemaphoreType.DMA((4,))
    w_qkv, w_out, *mixed = call(
        first_kernel,
        [shape(wq_dims), shape(wo_dims), shape(block, F32), shape(block), shape(block), shape(block)],
        [SMEM] + [VMEM] * 4 + [ANY] * 20,
        [
            pltpu.VMEM(wq_dims, BF16),
            pltpu.VMEM(wo_dims, BF16),
            pltpu.VMEM((rows, heads_width), BF16),
            pltpu.SemaphoreType.DMA((64,)),
            pltpu.SemaphoreType.DMA((64,)),
            pltpu.SemaphoreType.DMA((2,)),
        ],
        4 * project_flops // 3,
        (info, *x_first, *q_parts, *o_parts),
        [ANY] * 2 + [VMEM] * 4,
    )

    def finish(x_own, moments, stats, parts, own_grad):
        opposite = shift_tensor(parts[3], 2)
        arrived = [shift_tensor(parts[1], 1), shift_tensor(parts[2], -1), opposite]
        norm_grad = parts[0]
        plain, weighted = stats[:, 0:1], stats[:, 1:2]
        for part in arrived:
            part = part.astype(F32)
            norm_grad = norm_grad + part[:, :own_width]
            sums = part[:, own_width : own_width + 4]
            plain = plain + (sums[:, 0:1] + sums[:, 1:2])
            weighted = weighted + (sums[:, 2:3] + sums[:, 3:4])
        mean, inverse = moments[:, 0:1], moments[:, 1:2]
        unit = (x_own.astype(F32) - mean) * inverse
        centered = norm_grad - plain / width - unit * (weighted / width)
        return (own_grad.astype(F32) + inverse * centered).astype(BF16)

    opposite = shift_tensor(mixed[3], 2)
    arrived = [shift_tensor(mixed[1], 1), shift_tensor(mixed[2], -1), opposite]
    mixed_own = mixed[0] + sum(part.astype(F32) for part in arrived)
    first_out = (frames.astype(F32) + live_rows * mixed_own).astype(BF16)
    (grad_top,) = call(
        context_grad_kernel,
        [shape((rows, heads_width))],
        [SMEM] + [VMEM] * 4 + [ANY],
        [pltpu.VMEM(wo_dims, BF16), block_sems],
        project_flops // 3,
        (info, *g_first, w_out),
    )
    first_out, grad_top = lax.optimization_barrier((first_out, grad_top))

    entry = jnp.where(on_first, frames, cross_section(first_out, 0))
    x_entry = gather_tensor(entry)
    norm_outs = [shape((rows, 2), F32), shape(block, F32), shape(wide), shape(wide), shape(wide)]
    normed, qkv, attend, context, moments, stats, *parts = call(
        middle_kernel,
        [
            shape((4, *block)),
            shape((3, rows, heads_width)),
            shape((heads, rows, rows), F32),
            shape((rows, heads_width)),
            shape((rows, 2), F32),
        ]
        + norm_outs,
        [SMEM] + [VMEM] * 5 + [ANY],
        [pltpu.VMEM((3, rows, heads_width), BF16), pltpu.VMEM(wq_dims, BF16), block_sems],
        2 * project_flops,
        (info, *x_entry, grad_top, w_qkv),
    )
    upper_grad = finish(x_entry[0], moments, stats, parts, grad_out)
    top_grad = jnp.where(on_first, cross_section(upper_grad, 1), grad_out)
    q_part, o_part = shape((4, 2, 3, half, heads_width)), shape((4, 2, half, heads_width))
    gq, *blocks = call(
        last_kernel,
        [shape((3, rows, heads_width))] + [q_part] * 8 + [o_part] * 8,
        [SMEM] + [VMEM] * 4 + [ANY] + [VMEM] * 4,
        [
            pltpu.VMEM(wo_dims, BF16),
            pltpu.VMEM((4, *block), BF16),
            pltpu.VMEM((4, *wo_dims), BF16),
            block_sems,
        ],
        2 * project_flops,
        (info, *gather_tensor(top_grad), w_out, qkv, attend, normed, context),
    )
    q_sum = reduce_weights(blocks[0:4], blocks[4:8], "z", "y")
    o_sum = reduce_weights(blocks[8:12], blocks[12:16], "y", "z")
    stats, *parts = call(
        norm_kernel,
        norm_outs,
        [SMEM] + [VMEM] * 6 + [ANY],
        [pltpu.VMEM(wq_dims, BF16), block_sems],
        project_flops,
        (info, *x_entry, moments, gq, w_qkv),
    )
    grad_in = finish(x_entry[0], moments, stats, parts, top_grad)
    qkv_grad = q_sum.transpose(1, 0, 2, 3).reshape(1, 3, shard_rows, heads_width)
    out_grad = o_sum.reshape(shard_rows, heads_width).T[None]
    return (grad_in[None], qkv_grad, out_grad)


def solution(mesh):
    in_specs = (
        P("fsdp", "tensor"),
        P("fsdp"),
        P("section", None, "fsdp", "tensor"),
        P("section", "tensor", "fsdp"),
        P("fsdp", "tensor"),
    )
    out_specs = (
        P("section", "fsdp", "tensor"),
        P("section", None, "fsdp", "tensor"),
        P("section", "tensor", "fsdp"),
    )
    return jax.shard_map(local, mesh=mesh, in_specs=in_specs, out_specs=out_specs, check_vma=False)
```

```python
import jax
import jax.numpy as jnp
from jax import lax
from jax.experimental import pallas as pl
from jax.experimental.pallas import tpu as pltpu
from jax.sharding import PartitionSpec as P

HEAD = 128
EPSILON = 1e-05
F32 = jnp.float32
BF16 = jnp.bfloat16
VMEM_LIMIT = 56 << 20

REL_GET = (0, 3, 1, 2)
REL_PUT = (0, 1, 3, 2)


def shift_tensor(value, step):
    count = lax.axis_size("tensor")
    return lax.ppermute(value, "tensor", [(i, (i + step) % count) for i in range(count)])


def cross_section(value, source):
    return lax.ppermute(value, "section", [(source, 1 - source)])


def shift_grid(value, phase, step):
    pairs = []
    for section in range(2):
        along_z = (section == 1) == (phase == "near")
        for z in range(4):
            for y in range(4):
                for core in range(2):
                    to_z, to_y = ((z + step) % 4, y) if along_z else (z, (y + step) % 4)
                    pairs.append(
                        (section * 32 + z * 8 + y * 2 + core, section * 32 + to_z * 8 + to_y * 2 + core)
                    )
    return lax.ppermute(value, ("section", "fsdp"), pairs)


def swap_cores(value):
    count = lax.axis_size("fsdp")
    return lax.ppermute(value, "fsdp", [(i, i ^ 1) for i in range(count)])


def gather_tensor(own):
    opposite = shift_tensor(own, 2)
    return (own, shift_tensor(own, 1), shift_tensor(own, -1), opposite)


def ring_get(value, phase):
    half = value.shape[0] // 2
    behind, ahead = shift_grid(value, phase, 1), shift_grid(value, phase, -1)
    return behind, ahead, shift_grid(behind[:half], phase, 1), shift_grid(ahead[half:], phase, -1)


def gather_weights(shard):
    behind, ahead, low, high = ring_get(shard, "near")
    line = jnp.stack([shard, behind, ahead, jnp.concatenate([low, high], 0)])
    mine = (line, *ring_get(line, "far"))
    return mine + tuple(swap_cores(part) for part in mine)


def add(*terms):
    total = terms[0].astype(F32)
    for term in terms[1:]:
        total = total + term.astype(F32)
    return total.astype(BF16)


def ring_put(blocks, phase):
    own, ahead, behind, opposite = blocks
    half = own.shape[0] // 2
    low, high = shift_grid(opposite[:half], phase, 1), shift_grid(opposite[half:], phase, -1)
    ahead = jnp.concatenate([add(ahead[:half], low), ahead[half:]], 0)
    behind = jnp.concatenate([behind[:half], add(behind[half:], high)], 0)
    return add(own, shift_grid(ahead, phase, 1), shift_grid(behind, phase, -1))


def dot_nn(a, b):
    return jnp.dot(a, b, preferred_element_type=F32)


def dot_nt(a, b):
    return lax.dot_general(a, b, (((1,), (1,)), ((), ())), preferred_element_type=F32)


def dot_tn(a, b):
    return lax.dot_general(a, b, (((0,), (0,)), ((), ())), preferred_element_type=F32)


def block_of(info, rel):
    return lax.rem(info[0] + rel, 4)


def rows_of(ref, block, width):
    return ref[pl.ds(pl.multiple_of(block * width, width), width), :]


def live_column(info, rows):
    return lax.broadcasted_iota(jnp.int32, (rows, 1), 0) < info[5]


def row_moments(x_refs):
    width = sum(ref.shape[1] for ref in x_refs)
    total = sum(jnp.sum(ref[...].astype(F32), axis=-1, keepdims=True) for ref in x_refs)
    mean = total / width
    square = 0.0
    for ref in x_refs:
        centered = ref[...].astype(F32) - mean
        square = square + jnp.sum(centered * centered, axis=-1, keepdims=True)
    return mean, lax.rsqrt(square / width + EPSILON)


def project(info, x_refs, w_ref, mean, inverse, normed_ref=None, copies=None):
    totals = [None, None, None]
    for index, (rel, ref) in enumerate(zip(REL_GET, x_refs)):
        block = block_of(info, rel)
        normed = ((ref[...].astype(F32) - mean) * inverse).astype(BF16)
        if normed_ref is not None:
            normed_ref[block] = normed
        if copies is not None:
            copies[index].wait()
        for c in range(3):
            part = dot_nn(normed, rows_of(w_ref.at[c], block, ref.shape[1]))
            totals[c] = part if totals[c] is None else totals[c] + part
    return [total.astype(BF16) for total in totals]


def attend_head(info, queries, keys, values):
    rows = queries.shape[0]
    scores = dot_nt(queries, keys) * (float(HEAD) ** -0.5)
    live_keys = lax.broadcasted_iota(jnp.int32, (rows, rows), 1) < info[5]
    scores = jnp.where(live_keys, scores, F32(-1e30))
    raised = jnp.exp(scores - jnp.max(scores, axis=-1, keepdims=True))
    attend = raised / jnp.sum(raised, axis=-1, keepdims=True)
    return attend, dot_nn(attend.astype(BF16), values).astype(BF16)


def head_slices(width):
    return [slice(start, start + HEAD) for start in range(0, width, HEAD)]


def place_row(info, rel_near, rel_far, core, rows):
    rel_y = lax.select(info[4] == 0, rel_near, rel_far)
    rel_z = lax.select(info[4] == 0, rel_far, rel_near)
    z, y = lax.rem(info[1] + rel_z, 4), lax.rem(info[2] + rel_y, 4)
    return pl.multiple_of(((z * 4 + y) * 2 + core) * rows, rows)


def first_kernel(info, *refs):
    x_refs, parts = refs[:4], refs[4:14]
    wq_out, wo_out = refs[14:16]
    mixed_refs = refs[16:20]
    wq_ref, wo_ref, context_ref, q_sems, o_sems, out_sems = refs[20:]
    q_copies, o_copies = [], []
    rows = parts[0].shape[-2]
    for side in range(2):
        arrays = parts[side * 5 : side * 5 + 5]
        core = info[3] if side == 0 else 1 - info[3]
        for far, rel_far in enumerate(REL_GET):
            for near, rel_near in enumerate(REL_GET):
                source = arrays[far].at[near] if far < 3 else arrays[3 + near // 2].at[near % 2]
                place = pl.ds(place_row(info, rel_near, rel_far, core, rows), rows)
                number = len(q_copies)
                q_copies.append(
                    pltpu.make_async_copy(source.at[pl.ds(0, 3)], wq_ref.at[:, place, :], q_sems.at[number])
                )
                o_copies.append(pltpu.make_async_copy(source.at[3], wo_ref.at[place, :], o_sems.at[number]))
    for copy in q_copies + o_copies:
        copy.start()
    mean, inverse = row_moments(x_refs)
    for copy in q_copies:
        copy.wait()
    save_q = pltpu.make_async_copy(wq_ref, wq_out, out_sems.at[0])
    save_q.start()
    queries, keys, values = project(info, x_refs, wq_ref, mean, inverse)
    for copy in o_copies:
        copy.wait()
    save_o = pltpu.make_async_copy(wo_ref, wo_out, out_sems.at[1])
    save_o.start()
    for cols in head_slices(queries.shape[1]):
        _, context_ref[:, cols] = attend_head(info, queries[:, cols], keys[:, cols], values[:, cols])
    context = context_ref[...]
    for rel, ref in zip(REL_PUT, mixed_refs):
        ref[...] = dot_nt(context, rows_of(wo_ref, block_of(info, rel), ref.shape[1])).astype(ref.dtype)
    save_q.wait()
    save_o.wait()


def load_blocks(info, order, w_hbm, w_ref, sems):
    width = w_ref.shape[-2] // 4
    copies = []
    for rel in order:
        rows = pl.ds(pl.multiple_of(block_of(info, rel) * width, width), width)
        where = (slice(None), rows) if len(w_ref.shape) == 3 else (rows,)
        copies.append(pltpu.make_async_copy(w_hbm.at[where], w_ref.at[where], sems.at[len(copies)]))
    for copy in copies:
        copy.start()
    return copies


def context_grad(info, g_refs, w_ref, masked_ref=None, copies=None):
    live = live_column(info, g_refs[0].shape[0])
    total = None
    for index, (rel, ref) in enumerate(zip(REL_GET, g_refs)):
        block = block_of(info, rel)
        masked = jnp.where(live, ref[...].astype(F32), 0.0).astype(BF16)
        if masked_ref is not None:
            masked_ref[block] = masked
        if copies is not None:
            copies[index].wait()
        part = dot_nn(masked, rows_of(w_ref, block, ref.shape[1]))
        total = part if total is None else total + part
    return total.astype(BF16)


def context_grad_kernel(info, *refs):
    g_refs, w_hbm, grad_ref, w_ref, sems = refs[:4], refs[4], refs[5], refs[6], refs[7]
    copies = load_blocks(info, REL_GET, w_hbm, w_ref, sems)
    grad_ref[...] = context_grad(info, g_refs, w_ref, copies=copies)


def attend_backward(qkv_ref, attend_ref, grad, gq_ref):
    scale = float(HEAD) ** -0.5
    for head, cols in enumerate(head_slices(grad.shape[1])):
        grad_head = grad[:, cols]
        queries, keys, values = (qkv_ref[c, :, cols] for c in range(3))
        attend = attend_ref[head]
        grad_attend = dot_nt(grad_head, values)
        gq_ref[2, :, cols] = dot_tn(attend.astype(BF16), grad_head).astype(BF16)
        inner = jnp.sum(grad_attend * attend, axis=-1, keepdims=True)
        grad_scores = (attend * (grad_attend - inner) * scale).astype(BF16)
        gq_ref[0, :, cols] = dot_nn(grad_scores, keys).astype(BF16)
        gq_ref[1, :, cols] = dot_tn(grad_scores, queries).astype(BF16)


def norm_parts(info, x_refs, mean, inverse, gq_ref, w_ref, stat_ref, norm_refs, order, copies=None):
    width = x_refs[0].shape[1]
    plain, weighted = 0.0, 0.0
    by_rel = dict(zip(REL_GET, x_refs))
    out_by_rel = dict(zip(REL_PUT, norm_refs))
    for index, rel in enumerate(order):
        block = block_of(info, rel)
        if copies is not None:
            copies[index].wait()
        part = None
        for c in range(3):
            term = dot_nt(gq_ref[c], rows_of(w_ref.at[c], block, width))
            part = term if part is None else part + term
        unit = (by_rel[rel][...].astype(F32) - mean) * inverse
        plain = plain + jnp.sum(part, axis=-1, keepdims=True)
        weighted = weighted + jnp.sum(part * unit, axis=-1, keepdims=True)
        ref = out_by_rel[rel]
        ref[:, :width] = part.astype(ref.dtype)
    stat_ref[:, 0:1] = plain
    stat_ref[:, 1:2] = weighted
    lane = lax.broadcasted_iota(jnp.int32, (plain.shape[0], 128), 1)
    plain_high, weighted_high = plain.astype(BF16).astype(F32), weighted.astype(BF16).astype(F32)
    packed = jnp.where(lane == 0, plain_high, jnp.where(lane == 1, plain - plain_high, 0.0))
    packed = jnp.where(lane == 2, weighted_high, jnp.where(lane == 3, weighted - weighted_high, packed))
    for ref in norm_refs[1:]:
        ref[:, width:] = packed.astype(BF16)


def middle_kernel(info, *refs):
    x_refs, grad_ref, w_hbm = refs[:4], refs[4], refs[5]
    normed_ref, qkv_ref, attend_ref, context_ref, moment_ref, stat_ref = refs[6:12]
    norm_refs, gq_ref, w_ref, sems = refs[12:16], refs[16], refs[17], refs[18]
    copies = load_blocks(info, REL_GET, w_hbm, w_ref, sems)
    mean, inverse = row_moments(x_refs)
    moment_ref[:, 0:1] = mean
    moment_ref[:, 1:2] = inverse
    queries, keys, values = project(info, x_refs, w_ref, mean, inverse, normed_ref, copies)
    qkv_ref[0] = queries
    qkv_ref[1] = keys
    qkv_ref[2] = values
    for head, cols in enumerate(head_slices(queries.shape[1])):
        attend, context = attend_head(info, queries[:, cols], keys[:, cols], values[:, cols])
        attend_ref[head] = attend
        context_ref[:, cols] = context
    attend_backward(qkv_ref, attend_ref, grad_ref[...], gq_ref)
    norm_parts(info, x_refs, mean, inverse, gq_ref, w_ref, stat_ref, norm_refs, REL_PUT)


def norm_kernel(info, *refs):
    x_refs, moment_ref, gq_ref, w_hbm = refs[:4], refs[4], refs[5], refs[6]
    stat_ref, norm_refs, w_ref, sems = refs[7], refs[8:12], refs[12], refs[13]
    order = (2, 1, 3, 0)
    copies = load_blocks(info, order, w_hbm, w_ref, sems)
    mean, inverse = moment_ref[:, 0:1], moment_ref[:, 1:2]
    norm_parts(info, x_refs, mean, inverse, gq_ref, w_ref, stat_ref, norm_refs, order, copies)


def last_kernel(info, *refs):
    g_refs, w_hbm, qkv_ref, attend_ref, normed_ref, context_ref = refs[:4], *refs[4:9]
    gq_ref, outs = refs[9], refs[10:18]
    w_ref, masked_ref, block_ref, sems = refs[18:22]
    copies = load_blocks(info, REL_GET, w_hbm, w_ref, sems)
    grad = context_grad(info, g_refs, w_ref, masked_ref, copies)
    attend_backward(qkv_ref, attend_ref, grad, gq_ref)
    rows = outs[0].shape[-2]
    for c in range(4):
        for z in range(4):
            left = normed_ref[z] if c < 3 else masked_ref[z]
            right = gq_ref[c] if c < 3 else context_ref[...]
            block_ref[c, pl.ds(z * left.shape[1], left.shape[1]), :] = dot_tn(left, right).astype(BF16)
    for side in range(2):
        core = info[3] if side == 0 else 1 - info[3]
        for far, rel_far in enumerate(REL_PUT):
            for near, rel_near in enumerate(REL_PUT):
                place = pl.ds(place_row(info, rel_near, rel_far, core, rows), rows)
                for c in range(4):
                    outs[side * 4 + far][near, c] = block_ref[c, place, :]


VMEM = pl.BlockSpec(memory_space=pltpu.VMEM)
SMEM = pl.BlockSpec(memory_space=pltpu.SMEM)
ANY = pl.BlockSpec(memory_space=pl.ANY)


def call(kernel, outs, in_specs, scratch, flops, args, out_specs=None):
    moved = sum(a.size * a.dtype.itemsize for a in args)
    return pl.pallas_call(
        kernel,
        out_shape=outs,
        in_specs=in_specs,
        out_specs=out_specs or [VMEM] * len(outs),
        scratch_shapes=scratch,
        compiler_params=pltpu.CompilerParams(vmem_limit_bytes=VMEM_LIMIT),
        cost_estimate=pl.CostEstimate(flops=flops, bytes_accessed=moved, transcendentals=0),
    )(*args)


def shape(dims, dtype=BF16):
    return jax.ShapeDtypeStruct(dims, dtype)


def local(frames, lengths, qkv_weight, out_weight, grad_out):
    rows, own_width = frames.shape
    shard_rows, heads_width = qkv_weight.shape[2:]
    heads = heads_width // HEAD
    width = own_width * lax.axis_size("tensor")
    place = lax.axis_index("fsdp")
    section = lax.axis_index("section")
    on_first = section == 0
    info = jnp.stack(
        [lax.axis_index("tensor"), place // 8, place // 2 % 4, place % 2, section, lengths[0]]
    ).astype(jnp.int32)
    live_rows = (jnp.arange(rows, dtype=jnp.int32)[:, None] < lengths[0]).astype(F32)

    w_parts = gather_weights(jnp.concatenate([qkv_weight[0], out_weight[0].T[None]], 0))
    x_first, g_first = lax.optimization_barrier((gather_tensor(frames), gather_tensor(grad_out)))

    block = (rows, own_width)
    wide = (rows, own_width + 128)
    wq_dims, wo_dims = (3, width, heads_width), (width, heads_width)
    project_flops = 2 * rows * width * 3 * heads_width
    block_sems = pltpu.SemaphoreType.DMA((4,))
    w_qkv, w_out, *mixed = call(
        first_kernel,
        [shape(wq_dims), shape(wo_dims), shape(block, F32), shape(block), shape(block), shape(block)],
        [SMEM] + [VMEM] * 4 + [ANY] * 10,
        [
            pltpu.VMEM(wq_dims, BF16),
            pltpu.VMEM(wo_dims, BF16),
            pltpu.VMEM((rows, heads_width), BF16),
            pltpu.SemaphoreType.DMA((32,)),
            pltpu.SemaphoreType.DMA((32,)),
            pltpu.SemaphoreType.DMA((2,)),
        ],
        4 * project_flops // 3,
        (info, *x_first, *w_parts),
        [ANY] * 2 + [VMEM] * 4,
    )

    def finish(x_own, moments, stats, parts, own_grad):
        opposite = shift_tensor(parts[3], 2)
        arrived = [shift_tensor(parts[1], 1), shift_tensor(parts[2], -1), opposite]
        norm_grad = parts[0]
        plain, weighted = stats[:, 0:1], stats[:, 1:2]
        for part in arrived:
            part = part.astype(F32)
            norm_grad = norm_grad + part[:, :own_width]
            sums = part[:, own_width : own_width + 4]
            plain = plain + (sums[:, 0:1] + sums[:, 1:2])
            weighted = weighted + (sums[:, 2:3] + sums[:, 3:4])
        mean, inverse = moments[:, 0:1], moments[:, 1:2]
        unit = (x_own.astype(F32) - mean) * inverse
        centered = norm_grad - plain / width - unit * (weighted / width)
        return (own_grad.astype(F32) + inverse * centered).astype(BF16)

    opposite = shift_tensor(mixed[3], 2)
    arrived = [shift_tensor(mixed[1], 1), shift_tensor(mixed[2], -1), opposite]
    mixed_own = mixed[0] + sum(part.astype(F32) for part in arrived)
    first_out = (frames.astype(F32) + live_rows * mixed_own).astype(BF16)
    (grad_top,) = call(
        context_grad_kernel,
        [shape((rows, heads_width))],
        [SMEM] + [VMEM] * 4 + [ANY],
        [pltpu.VMEM(wo_dims, BF16), block_sems],
        project_flops // 3,
        (info, *g_first, w_out),
    )
    first_out, grad_top = lax.optimization_barrier((first_out, grad_top))

    entry = jnp.where(on_first, frames, cross_section(first_out, 0))
    x_entry = gather_tensor(entry)
    norm_outs = [shape((rows, 2), F32), shape(block, F32), shape(wide), shape(wide), shape(wide)]
    normed, qkv, attend, context, moments, stats, *parts = call(
        middle_kernel,
        [
            shape((4, *block)),
            shape((3, rows, heads_width)),
            shape((heads, rows, rows), F32),
            shape((rows, heads_width)),
            shape((rows, 2), F32),
        ]
        + norm_outs,
        [SMEM] + [VMEM] * 5 + [ANY],
        [pltpu.VMEM((3, rows, heads_width), BF16), pltpu.VMEM(wq_dims, BF16), block_sems],
        2 * project_flops,
        (info, *x_entry, grad_top, w_qkv),
    )
    upper_grad = finish(x_entry[0], moments, stats, parts, grad_out)
    top_grad = jnp.where(on_first, cross_section(upper_grad, 1), grad_out)
    gq, *blocks = call(
        last_kernel,
        [shape((3, rows, heads_width))] + [shape((4, 4, shard_rows, heads_width))] * 8,
        [SMEM] + [VMEM] * 4 + [ANY] + [VMEM] * 4,
        [
            pltpu.VMEM(wo_dims, BF16),
            pltpu.VMEM((4, *block), BF16),
            pltpu.VMEM((4, *wo_dims), BF16),
            block_sems,
        ],
        2 * project_flops,
        (info, *gather_tensor(top_grad), w_out, qkv, attend, normed, context),
    )
    order = (3, 1, 2, 0)
    arrived = {i: swap_cores(blocks[4 + i]) for i in order}
    gq, arrived[3] = lax.optimization_barrier((gq, arrived[3]))
    line = ring_put([add(blocks[i], arrived[i]) for i in range(4)], "far")
    weight_grad = ring_put([line[i] for i in range(4)], "near")
    stats, *parts = call(
        norm_kernel,
        norm_outs,
        [SMEM] + [VMEM] * 6 + [ANY],
        [pltpu.VMEM(wq_dims, BF16), block_sems],
        project_flops,
        (info, *x_entry, moments, gq, w_qkv),
    )
    grad_in = finish(x_entry[0], moments, stats, parts, top_grad)
    return (grad_in[None], weight_grad[None, :3], weight_grad[3].T[None])


def solution(mesh):
    in_specs = (
        P("fsdp", "tensor"),
        P("fsdp"),
        P("section", None, "fsdp", "tensor"),
        P("section", "tensor", "fsdp"),
        P("fsdp", "tensor"),
    )
    out_specs = (
        P("section", "fsdp", "tensor"),
        P("section", None, "fsdp", "tensor"),
        P("section", "tensor", "fsdp"),
    )
    return jax.shard_map(local, mesh=mesh, in_specs=in_specs, out_specs=out_specs, check_vma=False)
```

```python
import jax
import jax.numpy as jnp
from jax import lax
from jax.experimental import pallas as pl
from jax.experimental.pallas import tpu as pltpu
from jax.sharding import PartitionSpec as P

HEAD = 128
EPSILON = 1e-05
F32 = jnp.float32
BF16 = jnp.bfloat16

REL_GET = (0, 3, 1, 2)
REL_PUT = (0, 1, 3, 2)

REDUCE_FAR = "yz"
REDUCE_NEAR = "zy"


def shift_tensor(value, step):
    count = lax.axis_size("tensor")
    return lax.ppermute(value, "tensor", [(i, (i + step) % count) for i in range(count)])


def cross_section(value, source):
    return lax.ppermute(value, "section", [(source, 1 - source)])


def shift_grid(value, axes, step):
    pairs = []
    for section in range(2):
        for z in range(4):
            for y in range(4):
                for core in range(2):
                    to_z, to_y = ((z + step) % 4, y) if axes[section] == "z" else (z, (y + step) % 4)
                    pairs.append(
                        (section * 32 + z * 8 + y * 2 + core, section * 32 + to_z * 8 + to_y * 2 + core)
                    )
    return lax.ppermute(value, ("section", "fsdp"), pairs)


def swap_cores(value):
    count = lax.axis_size("fsdp")
    return lax.ppermute(value, "fsdp", [(i, i ^ 1) for i in range(count)])


def gather_tensor(own):
    opposite = shift_tensor(own, 2)
    return (own, shift_tensor(own, 1), shift_tensor(own, -1), opposite)


def ring_get(value, axes):
    half = value.shape[0] // 2
    behind, ahead = shift_grid(value, axes, 1), shift_grid(value, axes, -1)
    return behind, ahead, shift_grid(behind[:half], axes, 1), shift_grid(ahead[half:], axes, -1)


def gather_weights(shard):
    behind, ahead, low, high = ring_get(shard, "zz")
    line = jnp.stack([shard, behind, ahead, jnp.concatenate([low, high], 0)])
    mine = (line, *ring_get(line, "yy"))
    return mine + tuple(swap_cores(part) for part in mine)


def add(*terms):
    total = terms[0].astype(F32)
    for term in terms[1:]:
        total = total + term.astype(F32)
    return total.astype(BF16)


def ring_put(blocks, axes):
    own, ahead, behind, opposite = blocks
    half = own.shape[0] // 2
    low, high = shift_grid(opposite[:half], axes, 1), shift_grid(opposite[half:], axes, -1)
    ahead = jnp.concatenate([add(ahead[:half], low), ahead[half:]], 0)
    behind = jnp.concatenate([behind[:half], add(behind[half:], high)], 0)
    return add(own, shift_grid(ahead, axes, 1), shift_grid(behind, axes, -1))


def dot_nn(a, b):
    return jnp.dot(a, b, preferred_element_type=F32)


def dot_nt(a, b):
    return lax.dot_general(a, b, (((1,), (1,)), ((), ())), preferred_element_type=F32)


def dot_tn(a, b):
    return lax.dot_general(a, b, (((0,), (0,)), ((), ())), preferred_element_type=F32)


def block_of(info, rel):
    return lax.rem(info[0] + rel, 4)


def rows_of(ref, block, width):
    return ref[pl.ds(pl.multiple_of(block * width, width), width), :]


def live_column(info, rows):
    return lax.broadcasted_iota(jnp.int32, (rows, 1), 0) < info[5]


def row_moments(x_refs):
    width = sum(ref.shape[1] for ref in x_refs)
    total = sum(jnp.sum(ref[...].astype(F32), axis=-1, keepdims=True) for ref in x_refs)
    mean = total / width
    square = 0.0
    for ref in x_refs:
        centered = ref[...].astype(F32) - mean
        square = square + jnp.sum(centered * centered, axis=-1, keepdims=True)
    return mean, lax.rsqrt(square / width + EPSILON)


def project(info, x_refs, w_ref, mean, inverse, normed_ref=None):
    totals = [None, None, None]
    for rel, ref in zip(REL_GET, x_refs):
        block = block_of(info, rel)
        normed = ((ref[...].astype(F32) - mean) * inverse).astype(BF16)
        if normed_ref is not None:
            normed_ref[block] = normed
        for c in range(3):
            part = dot_nn(normed, rows_of(w_ref.at[c], block, ref.shape[1]))
            totals[c] = part if totals[c] is None else totals[c] + part
    return [total.astype(BF16) for total in totals]


def attend_head(info, queries, keys, values):
    rows = queries.shape[0]
    scores = dot_nt(queries, keys) * (float(HEAD) ** -0.5)
    live_keys = lax.broadcasted_iota(jnp.int32, (rows, rows), 1) < info[5]
    scores = jnp.where(live_keys, scores, F32(-1e30))
    raised = jnp.exp(scores - jnp.max(scores, axis=-1, keepdims=True))
    attend = raised / jnp.sum(raised, axis=-1, keepdims=True)
    return attend, dot_nn(attend.astype(BF16), values).astype(BF16)


def head_slices(width):
    return [slice(start, start + HEAD) for start in range(0, width, HEAD)]


def place_row(info, rel_z, rel_y, core, rows):
    z, y = lax.rem(info[1] + rel_z, 4), lax.rem(info[2] + rel_y, 4)
    return pl.multiple_of(((z * 4 + y) * 2 + core) * rows, rows)


def first_kernel(info, *refs):
    x_refs, parts = refs[:4], refs[4:14]
    wq_ref, wo_ref = refs[14:16]
    mixed_refs = refs[16:20]
    context_ref, q_sems, o_sems = refs[20:]
    q_copies, o_copies = [], []
    rows = parts[0].shape[-2]
    for side in range(2):
        arrays = parts[side * 5 : side * 5 + 5]
        core = info[3] if side == 0 else 1 - info[3]
        for far, rel_far in enumerate(REL_GET):
            for near, rel_near in enumerate(REL_GET):
                source = arrays[far].at[near] if far < 3 else arrays[3 + near // 2].at[near % 2]
                place = pl.ds(place_row(info, rel_near, rel_far, core, rows), rows)
                number = len(q_copies)
                q_copies.append(
                    pltpu.make_async_copy(source.at[pl.ds(0, 3)], wq_ref.at[:, place, :], q_sems.at[number])
                )
                o_copies.append(pltpu.make_async_copy(source.at[3], wo_ref.at[place, :], o_sems.at[number]))
    for copy in q_copies + o_copies:
        copy.start()
    mean, inverse = row_moments(x_refs)
    for copy in q_copies:
        copy.wait()
    queries, keys, values = project(info, x_refs, wq_ref, mean, inverse)
    for copy in o_copies:
        copy.wait()
    for cols in head_slices(queries.shape[1]):
        _, context_ref[:, cols] = attend_head(info, queries[:, cols], keys[:, cols], values[:, cols])
    context = context_ref[...]
    for rel, ref in zip(REL_PUT, mixed_refs):
        ref[...] = dot_nt(context, rows_of(wo_ref, block_of(info, rel), ref.shape[1])).astype(ref.dtype)


def context_grad(info, g_refs, w_ref, masked_ref=None):
    live = live_column(info, g_refs[0].shape[0])
    total = None
    for rel, ref in zip(REL_GET, g_refs):
        block = block_of(info, rel)
        masked = jnp.where(live, ref[...].astype(F32), 0.0).astype(BF16)
        if masked_ref is not None:
            masked_ref[block] = masked
        part = dot_nn(masked, rows_of(w_ref, block, ref.shape[1]))
        total = part if total is None else total + part
    return total.astype(BF16)


def context_grad_kernel(info, *refs):
    g_refs, w_ref, grad_ref = refs[:4], refs[4], refs[5]
    grad_ref[...] = context_grad(info, g_refs, w_ref)


def attend_backward(qkv_ref, attend_ref, grad, gq_ref):
    scale = float(HEAD) ** -0.5
    for head, cols in enumerate(head_slices(grad.shape[1])):
        grad_head = grad[:, cols]
        queries, keys, values = (qkv_ref[c, :, cols] for c in range(3))
        attend = attend_ref[head]
        grad_attend = dot_nt(grad_head, values)
        gq_ref[2, :, cols] = dot_tn(attend.astype(BF16), grad_head).astype(BF16)
        inner = jnp.sum(grad_attend * attend, axis=-1, keepdims=True)
        grad_scores = (attend * (grad_attend - inner) * scale).astype(BF16)
        gq_ref[0, :, cols] = dot_nn(grad_scores, keys).astype(BF16)
        gq_ref[1, :, cols] = dot_tn(grad_scores, queries).astype(BF16)


def norm_parts(info, x_refs, mean, inverse, gq_ref, w_ref, stat_ref, norm_refs):
    width = x_refs[0].shape[1]
    plain, weighted = 0.0, 0.0
    by_rel = dict(zip(REL_GET, x_refs))
    out_by_rel = dict(zip(REL_PUT, norm_refs))
    for rel in REL_PUT:
        block = block_of(info, rel)
        part = None
        for c in range(3):
            term = dot_nt(gq_ref[c], rows_of(w_ref.at[c], block, width))
            part = term if part is None else part + term
        unit = (by_rel[rel][...].astype(F32) - mean) * inverse
        plain = plain + jnp.sum(part, axis=-1, keepdims=True)
        weighted = weighted + jnp.sum(part * unit, axis=-1, keepdims=True)
        ref = out_by_rel[rel]
        ref[:, :width] = part.astype(ref.dtype)
    stat_ref[:, 0:1] = plain
    stat_ref[:, 1:2] = weighted
    lane = lax.broadcasted_iota(jnp.int32, (plain.shape[0], 128), 1)
    plain_high, weighted_high = plain.astype(BF16).astype(F32), weighted.astype(BF16).astype(F32)
    packed = jnp.where(lane == 0, plain_high, jnp.where(lane == 1, plain - plain_high, 0.0))
    packed = jnp.where(lane == 2, weighted_high, jnp.where(lane == 3, weighted - weighted_high, packed))
    for ref in norm_refs[1:]:
        ref[:, width:] = packed.astype(BF16)


def middle_kernel(info, *refs):
    x_refs, grad_ref, w_ref = refs[:4], refs[4], refs[5]
    normed_ref, qkv_ref, attend_ref, context_ref, moment_ref, stat_ref = refs[6:12]
    norm_refs, gq_ref = refs[12:16], refs[16]
    mean, inverse = row_moments(x_refs)
    moment_ref[:, 0:1] = mean
    moment_ref[:, 1:2] = inverse
    queries, keys, values = project(info, x_refs, w_ref, mean, inverse, normed_ref)
    qkv_ref[0] = queries
    qkv_ref[1] = keys
    qkv_ref[2] = values
    for head, cols in enumerate(head_slices(queries.shape[1])):
        attend, context = attend_head(info, queries[:, cols], keys[:, cols], values[:, cols])
        attend_ref[head] = attend
        context_ref[:, cols] = context
    attend_backward(qkv_ref, attend_ref, grad_ref[...], gq_ref)
    norm_parts(info, x_refs, mean, inverse, gq_ref, w_ref, stat_ref, norm_refs)


def norm_kernel(info, *refs):
    x_refs, moment_ref, gq_ref, w_ref = refs[:4], refs[4], refs[5], refs[6]
    stat_ref, norm_refs = refs[7], refs[8:12]
    mean, inverse = moment_ref[:, 0:1], moment_ref[:, 1:2]
    norm_parts(info, x_refs, mean, inverse, gq_ref, w_ref, stat_ref, norm_refs)


def last_kernel(info, *refs):
    g_refs, w_ref, qkv_ref, attend_ref, normed_ref, context_ref = refs[:4], *refs[4:9]
    gq_ref, outs = refs[9], refs[10:18]
    masked_ref, block_ref = refs[18:20]
    grad = context_grad(info, g_refs, w_ref, masked_ref)
    attend_backward(qkv_ref, attend_ref, grad, gq_ref)
    rows = outs[0].shape[-2]
    for c in range(4):
        for z in range(4):
            left = normed_ref[z] if c < 3 else masked_ref[z]
            right = gq_ref[c] if c < 3 else context_ref[...]
            block_ref[c, pl.ds(z * left.shape[1], left.shape[1]), :] = dot_tn(left, right).astype(BF16)
    for side in range(2):
        core = info[3] if side == 0 else 1 - info[3]
        for far, rel_far in enumerate(REL_PUT):
            for near, rel_near in enumerate(REL_PUT):
                rel_z = lax.select(info[4] == 0, rel_near, rel_far)
                rel_y = lax.select(info[4] == 0, rel_far, rel_near)
                place = pl.ds(place_row(info, rel_z, rel_y, core, rows), rows)
                for c in range(4):
                    outs[side * 4 + far][near, c] = block_ref[c, place, :]


VMEM = pl.BlockSpec(memory_space=pltpu.VMEM)
SMEM = pl.BlockSpec(memory_space=pltpu.SMEM)
ANY = pl.BlockSpec(memory_space=pl.ANY)


def call(kernel, outs, in_specs, scratch, flops, args, megabytes, out_specs=None):
    moved = sum(a.size * a.dtype.itemsize for a in args)
    return pl.pallas_call(
        kernel,
        out_shape=outs,
        in_specs=in_specs,
        out_specs=out_specs or [VMEM] * len(outs),
        scratch_shapes=scratch,
        compiler_params=pltpu.CompilerParams(vmem_limit_bytes=megabytes << 20),
        cost_estimate=pl.CostEstimate(flops=flops, bytes_accessed=moved, transcendentals=0),
    )(*args)


def shape(dims, dtype=BF16):
    return jax.ShapeDtypeStruct(dims, dtype)


def local(frames, lengths, qkv_weight, out_weight, grad_out):
    rows, own_width = frames.shape
    shard_rows, heads_width = qkv_weight.shape[2:]
    heads = heads_width // HEAD
    width = own_width * lax.axis_size("tensor")
    place = lax.axis_index("fsdp")
    section = lax.axis_index("section")
    on_first = section == 0
    info = jnp.stack(
        [lax.axis_index("tensor"), place // 8, place // 2 % 4, place % 2, section, lengths[0]]
    ).astype(jnp.int32)
    live_rows = (jnp.arange(rows, dtype=jnp.int32)[:, None] < lengths[0]).astype(F32)

    w_parts = gather_weights(jnp.concatenate([qkv_weight[0], out_weight[0].T[None]], 0))
    x_first, g_first = lax.optimization_barrier((gather_tensor(frames), gather_tensor(grad_out)))

    block = (rows, own_width)
    wide = (rows, own_width + 128)
    wq_dims, wo_dims = (3, width, heads_width), (width, heads_width)
    project_flops = 2 * rows * width * 3 * heads_width
    w_qkv, w_out, *mixed = call(
        first_kernel,
        [shape(wq_dims), shape(wo_dims), shape(block, F32), shape(block), shape(block), shape(block)],
        [SMEM] + [VMEM] * 4 + [ANY] * 10,
        [
            pltpu.VMEM((rows, heads_width), BF16),
            pltpu.SemaphoreType.DMA((32,)),
            pltpu.SemaphoreType.DMA((32,)),
        ],
        4 * project_flops // 3,
        (info, *x_first, *w_parts),
        16,
    )

    def finish(x_own, moments, stats, parts, own_grad):
        opposite = shift_tensor(parts[3], 2)
        arrived = [shift_tensor(parts[1], 1), shift_tensor(parts[2], -1), opposite]
        norm_grad = parts[0]
        plain, weighted = stats[:, 0:1], stats[:, 1:2]
        for part in arrived:
            part = part.astype(F32)
            norm_grad = norm_grad + part[:, :own_width]
            sums = part[:, own_width : own_width + 4]
            plain = plain + (sums[:, 0:1] + sums[:, 1:2])
            weighted = weighted + (sums[:, 2:3] + sums[:, 3:4])
        mean, inverse = moments[:, 0:1], moments[:, 1:2]
        unit = (x_own.astype(F32) - mean) * inverse
        centered = norm_grad - plain / width - unit * (weighted / width)
        return (own_grad.astype(F32) + inverse * centered).astype(BF16)

    opposite = shift_tensor(mixed[3], 2)
    arrived = [shift_tensor(mixed[1], 1), shift_tensor(mixed[2], -1), opposite]
    mixed_own = mixed[0] + sum(part.astype(F32) for part in arrived)
    first_out = (frames.astype(F32) + live_rows * mixed_own).astype(BF16)
    (grad_top,) = call(
        context_grad_kernel,
        [shape((rows, heads_width))],
        [SMEM] + [VMEM] * 5,
        [],
        project_flops // 3,
        (info, *g_first, w_out),
        16,
    )
    first_out, grad_top = lax.optimization_barrier((first_out, grad_top))

    entry = jnp.where(on_first, frames, cross_section(first_out, 0))
    x_entry = gather_tensor(entry)
    norm_outs = [shape((rows, 2), F32), shape(block, F32), shape(wide), shape(wide), shape(wide)]
    normed, qkv, attend, context, moments, stats, *parts = call(
        middle_kernel,
        [
            shape((4, *block)),
            shape((3, rows, heads_width)),
            shape((heads, rows, rows), F32),
            shape((rows, heads_width)),
            shape((rows, 2), F32),
        ]
        + norm_outs,
        [SMEM] + [VMEM] * 6,
        [pltpu.VMEM((3, rows, heads_width), BF16)],
        2 * project_flops,
        (info, *x_entry, grad_top, w_qkv),
        16,
    )
    upper_grad = finish(x_entry[0], moments, stats, parts, grad_out)
    top_grad = jnp.where(on_first, cross_section(upper_grad, 1), grad_out)
    gq, *blocks = call(
        last_kernel,
        [shape((3, rows, heads_width))] + [shape((4, 4, shard_rows, heads_width))] * 8,
        [SMEM] + [VMEM] * 9,
        [pltpu.VMEM((4, *block), BF16), pltpu.VMEM((4, *wo_dims), BF16)],
        2 * project_flops,
        (info, *gather_tensor(top_grad), w_out, qkv, attend, normed, context),
        28,
    )
    order = (3, 1, 2, 0)
    arrived = {i: swap_cores(blocks[4 + i]) for i in order}
    gq, arrived[3] = lax.optimization_barrier((gq, arrived[3]))
    line = ring_put([add(blocks[i], arrived[i]) for i in range(4)], REDUCE_FAR)
    weight_grad = ring_put([line[i] for i in range(4)], REDUCE_NEAR)
    stats, *parts = call(
        norm_kernel,
        norm_outs,
        [SMEM] + [VMEM] * 7,
        [],
        project_flops,
        (info, *x_entry, moments, gq, w_qkv),
        16,
    )
    grad_in = finish(x_entry[0], moments, stats, parts, top_grad)
    return (grad_in[None], weight_grad[None, :3], weight_grad[3].T[None])


def solution(mesh):
    in_specs = (
        P("fsdp", "tensor"),
        P("fsdp"),
        P("section", None, "fsdp", "tensor"),
        P("section", "tensor", "fsdp"),
        P("fsdp", "tensor"),
    )
    out_specs = (
        P("section", "fsdp", "tensor"),
        P("section", None, "fsdp", "tensor"),
        P("section", "tensor", "fsdp"),
    )
    return jax.shard_map(local, mesh=mesh, in_specs=in_specs, out_specs=out_specs, check_vma=False)
```

```python
import jax
import jax.numpy as jnp
from jax import lax
from jax.experimental import pallas as pl
from jax.experimental.pallas import tpu as pltpu
from jax.sharding import PartitionSpec as P

HEAD = 128
EPSILON = 1e-05
F32 = jnp.float32
BF16 = jnp.bfloat16

REL_GET = (0, 3, 1, 2)
REL_PUT = (0, 1, 3, 2)

NEAR, FAR = "yz", "zy"


def shift_tensor(value, step):
    count = lax.axis_size("tensor")
    return lax.ppermute(value, "tensor", [(i, (i + step) % count) for i in range(count)])


def cross_section(value, source):
    return lax.ppermute(value, "section", [(source, 1 - source)])


def shift_grid(value, axes, step):
    pairs = []
    for section in range(2):
        for z in range(4):
            for y in range(4):
                for core in range(2):
                    to_z, to_y = ((z + step) % 4, y) if axes[section] == "z" else (z, (y + step) % 4)
                    pairs.append(
                        (section * 32 + z * 8 + y * 2 + core, section * 32 + to_z * 8 + to_y * 2 + core)
                    )
    return lax.ppermute(value, ("section", "fsdp"), pairs)


def swap_cores(value):
    count = lax.axis_size("fsdp")
    return lax.ppermute(value, "fsdp", [(i, i ^ 1) for i in range(count)])


def gather_tensor(own):
    opposite = shift_tensor(own, 2)
    return (own, shift_tensor(own, 1), shift_tensor(own, -1), opposite)


def gather_weights(shard, x_own, g_own):
    opposite = shift_grid(shard, NEAR, 2)
    behind, ahead = shift_grid(shard, NEAR, 1), shift_grid(shard, NEAR, -1)
    x_pieces = gather_tensor(x_own)
    opposite, behind, ahead, x_pieces = lax.optimization_barrier((opposite, behind, ahead, x_pieces))
    line = jnp.stack([shard, behind, ahead, opposite])
    behind, ahead = shift_grid(line, FAR, 1), shift_grid(line, FAR, -1)
    g_pieces = gather_tensor(lax.optimization_barrier((g_own, line))[0])
    behind, ahead, g_pieces = lax.optimization_barrier((behind, ahead, g_pieces))
    low, high = shift_grid(behind[:2], FAR, 1), shift_grid(ahead[2:], FAR, -1)
    mine = (line, behind, ahead, low, high)
    return mine + tuple(swap_cores(part) for part in mine), x_pieces, g_pieces


def add(*terms):
    total = terms[0].astype(F32)
    for term in terms[1:]:
        total = total + term.astype(F32)
    return total.astype(BF16)


def ring_put(pairs, axes):
    own, ahead, behind, opposite = pairs
    low = shift_grid(add(*(term[0] for term in opposite)), axes, 1)
    high = shift_grid(add(*(term[1] for term in opposite)), axes, -1)
    ahead = jnp.stack([add(*(term[0] for term in ahead), low), add(*(term[1] for term in ahead))])
    behind = jnp.stack([add(*(term[0] for term in behind)), add(*(term[1] for term in behind), high)])
    return (*own, shift_grid(ahead, axes, 1), shift_grid(behind, axes, -1))


def reduce_weights(blocks):
    travel, own = blocks[0:4], blocks[4]
    far_opposite, far_rest, far_own = blocks[5:8]
    far_opposite = swap_cores(far_opposite)
    far_rest = swap_cores(far_rest)
    far_own = swap_cores(far_own)
    other = [far_rest[0], far_rest[1], far_rest[2], far_opposite]
    line = add(*ring_put([(travel[i], other[i]) for i in range(4)], FAR))
    far_own, line = lax.optimization_barrier((far_own, line))
    kept = ring_put([(own[i], far_own[i]) for i in range(4)], FAR)
    arrived = ring_put([(), (line[:, 0],), (line[:, 1],), (line[:, 2],)], NEAR)
    return add(*kept, *arrived)


def dot_nn(a, b):
    return jnp.dot(a, b, preferred_element_type=F32)


def dot_nt(a, b):
    return lax.dot_general(a, b, (((1,), (1,)), ((), ())), preferred_element_type=F32)


def dot_tn(a, b):
    return lax.dot_general(a, b, (((0,), (0,)), ((), ())), preferred_element_type=F32)


def block_of(info, rel):
    return lax.rem(info[0] + rel, 4)


def rows_of(ref, block, width):
    return ref[pl.ds(pl.multiple_of(block * width, width), width), :]


def live_column(info, rows):
    return lax.broadcasted_iota(jnp.int32, (rows, 1), 0) < info[5]


def row_moments(x_refs):
    width = sum(ref.shape[1] for ref in x_refs)
    total = sum(jnp.sum(ref[...].astype(F32), axis=-1, keepdims=True) for ref in x_refs)
    mean = total / width
    square = 0.0
    for ref in x_refs:
        centered = ref[...].astype(F32) - mean
        square = square + jnp.sum(centered * centered, axis=-1, keepdims=True)
    return mean, lax.rsqrt(square / width + EPSILON)


def project(info, x_refs, w_ref, mean, inverse, normed_ref=None):
    totals = [None, None, None]
    for rel, ref in zip(REL_GET, x_refs):
        block = block_of(info, rel)
        normed = ((ref[...].astype(F32) - mean) * inverse).astype(BF16)
        if normed_ref is not None:
            normed_ref[block] = normed
        for c in range(3):
            part = dot_nn(normed, rows_of(w_ref.at[c], block, ref.shape[1]))
            totals[c] = part if totals[c] is None else totals[c] + part
    return [total.astype(BF16) for total in totals]


def attend_head(info, queries, keys, values):
    rows = queries.shape[0]
    scores = dot_nt(queries, keys) * (float(HEAD) ** -0.5)
    live_keys = lax.broadcasted_iota(jnp.int32, (rows, rows), 1) < info[5]
    scores = jnp.where(live_keys, scores, F32(-1e30))
    raised = jnp.exp(scores - jnp.max(scores, axis=-1, keepdims=True))
    attend = raised / jnp.sum(raised, axis=-1, keepdims=True)
    return attend, dot_nn(attend.astype(BF16), values).astype(BF16)


def head_slices(width):
    return [slice(start, start + HEAD) for start in range(0, width, HEAD)]


def place_row(info, rel_near, rel_far, core, rows):
    rel_y = lax.select(info[4] == 0, rel_near, rel_far)
    rel_z = lax.select(info[4] == 0, rel_far, rel_near)
    z, y = lax.rem(info[1] + rel_z, 4), lax.rem(info[2] + rel_y, 4)
    return pl.multiple_of(((z * 4 + y) * 2 + core) * rows, rows)


def start_all(sources, target_ref, sems):
    copies = [pltpu.make_async_copy(ref, target_ref.at[i], sems.at[i]) for i, ref in enumerate(sources)]
    for copy in copies:
        copy.start()
    return copies


def first_kernel(info, *refs):
    x_sources, parts = refs[:4], refs[4:14]
    wq_out, wo_out = refs[14:16]
    mixed_refs = refs[16:20]
    x_ref, wq_ref, wo_ref, context_ref, x_sems, q_sems, o_sems, out_sems = refs[20:]
    x_copies = start_all(x_sources, x_ref, x_sems)
    x_refs = [x_ref.at[i] for i in range(4)]
    q_copies, o_copies = [], []
    rows = parts[0].shape[-2]
    for side in range(2):
        arrays = parts[side * 5 : side * 5 + 5]
        core = info[3] if side == 0 else 1 - info[3]
        for far, rel_far in enumerate(REL_GET):
            for near, rel_near in enumerate(REL_GET):
                source = arrays[far].at[near] if far < 3 else arrays[3 + near // 2].at[near % 2]
                place = pl.ds(place_row(info, rel_near, rel_far, core, rows), rows)
                number = len(q_copies)
                q_copies.append(
                    pltpu.make_async_copy(source.at[pl.ds(0, 3)], wq_ref.at[:, place, :], q_sems.at[number])
                )
                o_copies.append(pltpu.make_async_copy(source.at[3], wo_ref.at[place, :], o_sems.at[number]))
    for copy in q_copies + o_copies:
        copy.start()
    for copy in x_copies:
        copy.wait()
    mean, inverse = row_moments(x_refs)
    for copy in q_copies:
        copy.wait()
    save_q = pltpu.make_async_copy(wq_ref, wq_out, out_sems.at[0])
    save_q.start()
    queries, keys, values = project(info, x_refs, wq_ref, mean, inverse)
    for copy in o_copies:
        copy.wait()
    save_o = pltpu.make_async_copy(wo_ref, wo_out, out_sems.at[1])
    save_o.start()
    for cols in head_slices(queries.shape[1]):
        _, context_ref[:, cols] = attend_head(info, queries[:, cols], keys[:, cols], values[:, cols])
    context = context_ref[...]
    for rel, ref in zip(REL_PUT, mixed_refs):
        ref[...] = dot_nt(context, rows_of(wo_ref, block_of(info, rel), ref.shape[1])).astype(ref.dtype)
    save_q.wait()
    save_o.wait()


def load_kernel(source_ref, target_ref, sem):
    copy = pltpu.make_async_copy(source_ref, target_ref, sem)
    copy.start()
    copy.wait()


def context_grad(info, g_refs, w_ref, masked_ref=None):
    live = live_column(info, g_refs[0].shape[0])
    total = None
    for rel, ref in zip(REL_GET, g_refs):
        block = block_of(info, rel)
        masked = jnp.where(live, ref[...].astype(F32), 0.0).astype(BF16)
        if masked_ref is not None:
            masked_ref[block] = masked
        part = dot_nn(masked, rows_of(w_ref, block, ref.shape[1]))
        total = part if total is None else total + part
    return total.astype(BF16)


def context_grad_kernel(info, *refs):
    g_sources, w_ref, grad_ref, g_ref, sems = refs[:4], refs[4], refs[5], refs[6], refs[7]
    for copy in start_all(g_sources, g_ref, sems):
        copy.wait()
    grad_ref[...] = context_grad(info, [g_ref.at[i] for i in range(4)], w_ref)


def attend_backward(qkv_ref, attend_ref, grad, gq_ref):
    scale = float(HEAD) ** -0.5
    for head, cols in enumerate(head_slices(grad.shape[1])):
        grad_head = grad[:, cols]
        queries, keys, values = (qkv_ref[c, :, cols] for c in range(3))
        attend = attend_ref[head]
        grad_attend = dot_nt(grad_head, values)
        gq_ref[2, :, cols] = dot_tn(attend.astype(BF16), grad_head).astype(BF16)
        inner = jnp.sum(grad_attend * attend, axis=-1, keepdims=True)
        grad_scores = (attend * (grad_attend - inner) * scale).astype(BF16)
        gq_ref[0, :, cols] = dot_nn(grad_scores, keys).astype(BF16)
        gq_ref[1, :, cols] = dot_tn(grad_scores, queries).astype(BF16)


def norm_parts(info, x_refs, mean, inverse, gq_ref, w_ref, stat_ref, norm_refs):
    width = x_refs[0].shape[1]
    plain, weighted = 0.0, 0.0
    by_rel = dict(zip(REL_GET, x_refs))
    out_by_rel = dict(zip(REL_PUT, norm_refs))
    for rel in REL_PUT:
        block = block_of(info, rel)
        part = None
        for c in range(3):
            term = dot_nt(gq_ref[c], rows_of(w_ref.at[c], block, width))
            part = term if part is None else part + term
        unit = (by_rel[rel][...].astype(F32) - mean) * inverse
        plain = plain + jnp.sum(part, axis=-1, keepdims=True)
        weighted = weighted + jnp.sum(part * unit, axis=-1, keepdims=True)
        ref = out_by_rel[rel]
        ref[:, :width] = part.astype(ref.dtype)
    stat_ref[:, 0:1] = plain
    stat_ref[:, 1:2] = weighted
    lane = lax.broadcasted_iota(jnp.int32, (plain.shape[0], 128), 1)
    plain_high, weighted_high = plain.astype(BF16).astype(F32), weighted.astype(BF16).astype(F32)
    packed = jnp.where(lane == 0, plain_high, jnp.where(lane == 1, plain - plain_high, 0.0))
    packed = jnp.where(lane == 2, weighted_high, jnp.where(lane == 3, weighted - weighted_high, packed))
    for ref in norm_refs[1:]:
        ref[:, width:] = packed.astype(BF16)


def middle_kernel(info, *refs):
    x_refs, grad_ref, w_ref = refs[:4], refs[4], refs[5]
    normed_ref, qkv_ref, attend_ref, context_ref, moment_ref, stat_ref = refs[6:12]
    norm_refs, gq_ref = refs[12:16], refs[16]
    mean, inverse = row_moments(x_refs)
    moment_ref[:, 0:1] = mean
    moment_ref[:, 1:2] = inverse
    queries, keys, values = project(info, x_refs, w_ref, mean, inverse, normed_ref)
    qkv_ref[0] = queries
    qkv_ref[1] = keys
    qkv_ref[2] = values
    for head, cols in enumerate(head_slices(queries.shape[1])):
        attend, context = attend_head(info, queries[:, cols], keys[:, cols], values[:, cols])
        attend_ref[head] = attend
        context_ref[:, cols] = context
    attend_backward(qkv_ref, attend_ref, grad_ref[...], gq_ref)
    norm_parts(info, x_refs, mean, inverse, gq_ref, w_ref, stat_ref, norm_refs)


def norm_kernel(info, *refs):
    x_refs, moment_ref, gq_ref, w_ref = refs[:4], refs[4], refs[5], refs[6]
    stat_ref, norm_refs = refs[7], refs[8:12]
    mean, inverse = moment_ref[:, 0:1], moment_ref[:, 1:2]
    norm_parts(info, x_refs, mean, inverse, gq_ref, w_ref, stat_ref, norm_refs)


def last_kernel(info, *refs):
    g_refs, w_ref, qkv_ref, attend_ref, normed_ref, context_ref = refs[:4], *refs[4:9]
    gq_ref, outs = refs[9], refs[10:18]
    masked_ref, block_ref = refs[18:20]
    grad = context_grad(info, g_refs, w_ref, masked_ref)
    attend_backward(qkv_ref, attend_ref, grad, gq_ref)
    rows = outs[0].shape[-2]
    for c in range(4):
        for z in range(4):
            left = normed_ref[z] if c < 3 else masked_ref[z]
            right = gq_ref[c] if c < 3 else context_ref[...]
            block_ref[c, pl.ds(z * left.shape[1], left.shape[1]), :] = dot_tn(left, right).astype(BF16)
    travel, own, other_opposite, other_rest, other_own = outs[0:4], *outs[4:8]
    for side in range(2):
        core = info[3] if side == 0 else 1 - info[3]
        for far, rel_far in enumerate(REL_PUT):
            for near, rel_near in enumerate(REL_PUT):
                place = pl.ds(place_row(info, rel_near, rel_far, core, rows), rows)
                for c in range(4):
                    value = block_ref[c, place, :]
                    at = (c // 2, near - 1, c % 2)
                    if near == 0:
                        (own if side == 0 else other_own)[far, c // 2, c % 2] = value
                    elif side == 0:
                        travel[far][at] = value
                    elif far == 3:
                        other_opposite[at] = value
                    else:
                        other_rest[(far, *at)] = value


VMEM = pl.BlockSpec(memory_space=pltpu.VMEM)
SMEM = pl.BlockSpec(memory_space=pltpu.SMEM)
ANY = pl.BlockSpec(memory_space=pl.ANY)


def call(kernel, outs, in_specs, scratch, flops, args, megabytes, out_specs=None):
    moved = sum(a.size * a.dtype.itemsize for a in args)
    return pl.pallas_call(
        kernel,
        out_shape=outs,
        in_specs=in_specs,
        out_specs=out_specs or [VMEM] * len(outs),
        scratch_shapes=scratch,
        compiler_params=pltpu.CompilerParams(vmem_limit_bytes=megabytes << 20),
        cost_estimate=pl.CostEstimate(flops=flops, bytes_accessed=moved, transcendentals=0),
    )(*args)


def shape(dims, dtype=BF16):
    return jax.ShapeDtypeStruct(dims, dtype)


def local(frames, lengths, qkv_weight, out_weight, grad_out):
    rows, own_width = frames.shape
    shard_rows, heads_width = qkv_weight.shape[2:]
    heads = heads_width // HEAD
    width = own_width * lax.axis_size("tensor")
    place = lax.axis_index("fsdp")
    section = lax.axis_index("section")
    on_first = section == 0
    info = jnp.stack(
        [lax.axis_index("tensor"), place // 8, place // 2 % 4, place % 2, section, lengths[0]]
    ).astype(jnp.int32)
    live_rows = (jnp.arange(rows, dtype=jnp.int32)[:, None] < lengths[0]).astype(F32)

    shard = jnp.concatenate([qkv_weight[0], out_weight[0].T[None]], 0)
    w_parts, x_first, g_first = gather_weights(shard, frames, grad_out)

    block = (rows, own_width)
    wide = (rows, own_width + 128)
    wq_dims, wo_dims = (3, width, heads_width), (width, heads_width)
    project_flops = 2 * rows * width * 3 * heads_width
    w_qkv, w_out, *mixed = call(
        first_kernel,
        [shape(wq_dims), shape(wo_dims), shape(block, F32), shape(block), shape(block), shape(block)],
        [SMEM] + [ANY] * 14,
        [
            pltpu.VMEM((4, *block), BF16),
            pltpu.VMEM(wq_dims, BF16),
            pltpu.VMEM(wo_dims, BF16),
            pltpu.VMEM((rows, heads_width), BF16),
            pltpu.SemaphoreType.DMA((4,)),
            pltpu.SemaphoreType.DMA((32,)),
            pltpu.SemaphoreType.DMA((32,)),
            pltpu.SemaphoreType.DMA((2,)),
        ],
        4 * project_flops // 3,
        (info, *x_first, *w_parts),
        56,
        [ANY] * 2 + [VMEM] * 4,
    )

    def finish(x_own, moments, stats, parts, own_grad):
        opposite = shift_tensor(parts[3], 2)
        arrived = [shift_tensor(parts[1], 1), shift_tensor(parts[2], -1), opposite]
        norm_grad = parts[0]
        plain, weighted = stats[:, 0:1], stats[:, 1:2]
        for part in arrived:
            part = part.astype(F32)
            norm_grad = norm_grad + part[:, :own_width]
            sums = part[:, own_width : own_width + 4]
            plain = plain + (sums[:, 0:1] + sums[:, 1:2])
            weighted = weighted + (sums[:, 2:3] + sums[:, 3:4])
        mean, inverse = moments[:, 0:1], moments[:, 1:2]
        unit = (x_own.astype(F32) - mean) * inverse
        centered = norm_grad - plain / width - unit * (weighted / width)
        return (own_grad.astype(F32) + inverse * centered).astype(BF16)

    opposite = shift_tensor(mixed[3], 2)
    arrived = [shift_tensor(mixed[1], 1), shift_tensor(mixed[2], -1), opposite]
    mixed_own = mixed[0] + sum(part.astype(F32) for part in arrived)
    first_out = (frames.astype(F32) + live_rows * mixed_own).astype(BF16)
    (grad_top,) = call(
        context_grad_kernel,
        [shape((rows, heads_width))],
        [SMEM] + [ANY] * 4 + [VMEM],
        [pltpu.VMEM((4, *block), BF16), pltpu.SemaphoreType.DMA((4,))],
        project_flops // 3,
        (info, *g_first, w_out),
        56,
    )
    first_out, grad_top = lax.optimization_barrier((first_out, grad_top))

    entry = jnp.where(on_first, frames, cross_section(first_out, 0))
    x_entry = gather_tensor(entry)
    (w_loaded,) = call(
        load_kernel,
        [shape(wq_dims)],
        [ANY],
        [pltpu.SemaphoreType.DMA(())],
        0,
        (lax.optimization_barrier((w_qkv, entry))[0],),
        8,
    )
    norm_outs = [shape((rows, 2), F32), shape(block, F32), shape(wide), shape(wide), shape(wide)]
    normed, qkv, attend, context, moments, stats, *parts = call(
        middle_kernel,
        [
            shape((4, *block)),
            shape((3, rows, heads_width)),
            shape((heads, rows, rows), F32),
            shape((rows, heads_width)),
            shape((rows, 2), F32),
        ]
        + norm_outs,
        [SMEM] + [VMEM] * 6,
        [pltpu.VMEM((3, rows, heads_width), BF16)],
        2 * project_flops,
        (info, *x_entry, grad_top, w_loaded),
        16,
    )
    upper_grad = finish(x_entry[0], moments, stats, parts, grad_out)
    top_grad = jnp.where(on_first, cross_section(upper_grad, 1), grad_out)
    size = (2, shard_rows, heads_width)
    travel, kept = (2, 3, *size), (4, 2, *size)
    gq, *blocks = call(
        last_kernel,
        [shape((3, rows, heads_width))]
        + [shape(travel)] * 4
        + [shape(kept), shape(travel), shape((3, *travel)), shape(kept)],
        [SMEM] + [VMEM] * 9,
        [pltpu.VMEM((4, *block), BF16), pltpu.VMEM((4, *wo_dims), BF16)],
        2 * project_flops,
        (info, *gather_tensor(top_grad), w_out, qkv, attend, normed, context),
        28,
    )
    weight_grad = reduce_weights(blocks).reshape(4, shard_rows, heads_width)
    gq = lax.optimization_barrier((gq, blocks))[0]
    stats, *parts = call(
        norm_kernel,
        norm_outs,
        [SMEM] + [VMEM] * 7,
        [],
        project_flops,
        (info, *x_entry, moments, gq, w_qkv),
        16,
    )
    grad_in = finish(x_entry[0], moments, stats, parts, top_grad)
    return (grad_in[None], weight_grad[None, :3], weight_grad[3].T[None])


def solution(mesh):
    in_specs = (
        P("fsdp", "tensor"),
        P("fsdp"),
        P("section", None, "fsdp", "tensor"),
        P("section", "tensor", "fsdp"),
        P("fsdp", "tensor"),
    )
    out_specs = (
        P("section", "fsdp", "tensor"),
        P("section", None, "fsdp", "tensor"),
        P("section", "tensor", "fsdp"),
    )
    return jax.shard_map(local, mesh=mesh, in_specs=in_specs, out_specs=out_specs, check_vma=False)
```

```python
import jax
import jax.numpy as jnp
from jax import lax
from jax.experimental import pallas as pl
from jax.experimental.pallas import tpu as pltpu
from jax.sharding import PartitionSpec as P

HEAD = 128
EPSILON = 1e-05
F32 = jnp.float32
BF16 = jnp.bfloat16

REL_GET = (0, 3, 1, 2)
REL_PUT = (0, 1, 3, 2)

NEAR, FAR = "zy", "yz"


def shift_tensor(value, step):
    count = lax.axis_size("tensor")
    return lax.ppermute(value, "tensor", [(i, (i + step) % count) for i in range(count)])


def cross_section(value, source):
    return lax.ppermute(value, "section", [(source, 1 - source)])


def shift_grid(value, axes, step):
    pairs = []
    for section in range(2):
        for z in range(4):
            for y in range(4):
                for core in range(2):
                    to_z, to_y = ((z + step) % 4, y) if axes[section] == "z" else (z, (y + step) % 4)
                    pairs.append(
                        (section * 32 + z * 8 + y * 2 + core, section * 32 + to_z * 8 + to_y * 2 + core)
                    )
    return lax.ppermute(value, ("section", "fsdp"), pairs)


def swap_cores(value):
    count = lax.axis_size("fsdp")
    return lax.ppermute(value, "fsdp", [(i, i ^ 1) for i in range(count)])


def gather_tensor(own):
    opposite = shift_tensor(own, 2)
    return (own, shift_tensor(own, 1), shift_tensor(own, -1), opposite)


def gather_weights(shard, x_own, g_own):
    opposite = shift_grid(shard, NEAR, 2)
    behind, ahead = shift_grid(shard, NEAR, 1), shift_grid(shard, NEAR, -1)
    x_pieces = gather_tensor(x_own)
    opposite, behind, ahead, x_pieces = lax.optimization_barrier((opposite, behind, ahead, x_pieces))
    ready = cross_section(opposite[0, :16, :128], 0)
    line = jnp.stack([shard, behind, ahead, opposite])
    line, ready, g_own = lax.optimization_barrier((line, ready, g_own))
    behind, ahead = shift_grid(line, FAR, 1), shift_grid(line, FAR, -1)
    g_pieces = gather_tensor(g_own)
    behind, ahead, g_pieces = lax.optimization_barrier((behind, ahead, g_pieces))
    low, high = shift_grid(behind[:2], FAR, 1), shift_grid(ahead[2:], FAR, -1)
    mine = (line, behind, ahead, low, high)
    return mine + tuple(swap_cores(part) for part in mine), x_pieces, g_pieces, ready


def add(*terms):
    total = terms[0].astype(F32)
    for term in terms[1:]:
        total = total + term.astype(F32)
    return total.astype(BF16)


def ring_put(blocks, axes):
    own, ahead, behind, opposite = blocks
    half = own.shape[0] // 2
    low, high = shift_grid(opposite[:half], axes, 1), shift_grid(opposite[half:], axes, -1)
    ahead = jnp.concatenate([add(ahead[:half], low), ahead[half:]], 0)
    behind = jnp.concatenate([behind[:half], add(behind[half:], high)], 0)
    return add(own, shift_grid(ahead, axes, 1), shift_grid(behind, axes, -1))


def dot_nn(a, b):
    return jnp.dot(a, b, preferred_element_type=F32)


def dot_nt(a, b):
    return lax.dot_general(a, b, (((1,), (1,)), ((), ())), preferred_element_type=F32)


def dot_tn(a, b):
    return lax.dot_general(a, b, (((0,), (0,)), ((), ())), preferred_element_type=F32)


def block_of(info, rel):
    return lax.rem(info[0] + rel, 4)


def rows_of(ref, block, width):
    return ref[pl.ds(pl.multiple_of(block * width, width), width), :]


def live_column(info, rows):
    return lax.broadcasted_iota(jnp.int32, (rows, 1), 0) < info[5]


def row_moments(x_refs):
    width = sum(ref.shape[1] for ref in x_refs)
    total = sum(jnp.sum(ref[...].astype(F32), axis=-1, keepdims=True) for ref in x_refs)
    mean = total / width
    square = 0.0
    for ref in x_refs:
        centered = ref[...].astype(F32) - mean
        square = square + jnp.sum(centered * centered, axis=-1, keepdims=True)
    return mean, lax.rsqrt(square / width + EPSILON)


def project(info, x_refs, w_ref, mean, inverse, normed_ref=None):
    totals = [None, None, None]
    for rel, ref in zip(REL_GET, x_refs):
        block = block_of(info, rel)
        normed = ((ref[...].astype(F32) - mean) * inverse).astype(BF16)
        if normed_ref is not None:
            normed_ref[block] = normed
        for c in range(3):
            part = dot_nn(normed, rows_of(w_ref.at[c], block, ref.shape[1]))
            totals[c] = part if totals[c] is None else totals[c] + part
    return [total.astype(BF16) for total in totals]


def attend_head(info, queries, keys, values):
    rows = queries.shape[0]
    scores = dot_nt(queries, keys) * (float(HEAD) ** -0.5)
    live_keys = lax.broadcasted_iota(jnp.int32, (rows, rows), 1) < info[5]
    scores = jnp.where(live_keys, scores, F32(-1e30))
    raised = jnp.exp(scores - jnp.max(scores, axis=-1, keepdims=True))
    attend = raised / jnp.sum(raised, axis=-1, keepdims=True)
    return attend, dot_nn(attend.astype(BF16), values).astype(BF16)


def head_slices(width):
    return [slice(start, start + HEAD) for start in range(0, width, HEAD)]


def place_row(info, rel_near, rel_far, core, rows):
    rel_z = lax.select(info[4] == 0, rel_near, rel_far)
    rel_y = lax.select(info[4] == 0, rel_far, rel_near)
    z, y = lax.rem(info[1] + rel_z, 4), lax.rem(info[2] + rel_y, 4)
    return pl.multiple_of(((z * 4 + y) * 2 + core) * rows, rows)


def start_all(sources, target_ref, sems):
    copies = [pltpu.make_async_copy(ref, target_ref.at[i], sems.at[i]) for i, ref in enumerate(sources)]
    for copy in copies:
        copy.start()
    return copies


def part_copies(info, parts, matrices, target_ref, sems):
    copies = []
    rows = parts[0].shape[-2]
    for side in range(2):
        core = info[3] if side == 0 else 1 - info[3]
        for far, rel_far in enumerate(REL_GET):
            for near, rel_near in enumerate(REL_GET):
                array = parts[side * 5 + (far if far < 3 else 3 + near // 2)]
                source = array.at[near if far < 3 else near % 2, matrices]
                place = pl.ds(place_row(info, rel_near, rel_far, core, rows), rows)
                target = target_ref.at[:, place, :] if isinstance(matrices, pl.Slice) else target_ref.at[place, :]
                copies.append(pltpu.make_async_copy(source, target, sems.at[len(copies)]))
    for copy in copies:
        copy.start()
    return copies


def first_kernel(info, *refs):
    x_sources, parts = refs[:4], refs[4:14]
    mixed_refs = refs[15:19]
    x_ref, wq_ref, wo_ref, context_ref, x_sems, q_sems, o_sems = refs[19:]
    x_copies = start_all(x_sources, x_ref, x_sems)
    x_refs = [x_ref.at[i] for i in range(4)]
    q_copies = part_copies(info, parts, pl.ds(0, 3), wq_ref, q_sems)
    o_copies = part_copies(info, parts, 3, wo_ref, o_sems)
    for copy in x_copies:
        copy.wait()
    mean, inverse = row_moments(x_refs)
    for copy in q_copies:
        copy.wait()
    queries, keys, values = project(info, x_refs, wq_ref, mean, inverse)
    for cols in head_slices(queries.shape[1]):
        _, context_ref[:, cols] = attend_head(info, queries[:, cols], keys[:, cols], values[:, cols])
    context = context_ref[...]
    for copy in o_copies:
        copy.wait()
    for rel, ref in zip(REL_PUT, mixed_refs):
        ref[...] = dot_nt(context, rows_of(wo_ref, block_of(info, rel), ref.shape[1])).astype(ref.dtype)


def load_kernel(source_ref, target_ref, sem):
    copy = pltpu.make_async_copy(source_ref, target_ref, sem)
    copy.start()
    copy.wait()


def context_grad(info, g_refs, w_ref, masked_ref=None):
    live = live_column(info, g_refs[0].shape[0])
    total = None
    for rel, ref in zip(REL_GET, g_refs):
        block = block_of(info, rel)
        masked = jnp.where(live, ref[...].astype(F32), 0.0).astype(BF16)
        if masked_ref is not None:
            masked_ref[block] = masked
        part = dot_nn(masked, rows_of(w_ref, block, ref.shape[1]))
        total = part if total is None else total + part
    return total.astype(BF16)


def context_grad_kernel(info, *refs):
    g_sources, parts, grad_ref, w_ref, wq_ref = refs[:4], refs[4:14], *refs[14:17]
    g_ref, g_sems, w_sems, q_sems = refs[17:]
    copies = start_all(g_sources, g_ref, g_sems) + part_copies(info, parts, 3, w_ref, w_sems)
    q_copies = part_copies(info, parts, pl.ds(0, 3), wq_ref, q_sems)
    for copy in copies:
        copy.wait()
    grad_ref[...] = context_grad(info, [g_ref.at[i] for i in range(4)], w_ref)
    for copy in q_copies:
        copy.wait()


def attend_backward(qkv_ref, attend_ref, grad, gq_ref):
    scale = float(HEAD) ** -0.5
    for head, cols in enumerate(head_slices(grad.shape[1])):
        grad_head = grad[:, cols]
        queries, keys, values = (qkv_ref[c, :, cols] for c in range(3))
        attend = attend_ref[head]
        grad_attend = dot_nt(grad_head, values)
        gq_ref[2, :, cols] = dot_tn(attend.astype(BF16), grad_head).astype(BF16)
        inner = jnp.sum(grad_attend * attend, axis=-1, keepdims=True)
        grad_scores = (attend * (grad_attend - inner) * scale).astype(BF16)
        gq_ref[0, :, cols] = dot_nn(grad_scores, keys).astype(BF16)
        gq_ref[1, :, cols] = dot_tn(grad_scores, queries).astype(BF16)


def norm_parts(info, x_refs, mean, inverse, gq_ref, w_ref, stat_ref, norm_refs):
    width = x_refs[0].shape[1]
    plain, weighted = 0.0, 0.0
    by_rel = dict(zip(REL_GET, x_refs))
    out_by_rel = dict(zip(REL_PUT, norm_refs))
    for rel in REL_PUT:
        block = block_of(info, rel)
        part = None
        for c in range(3):
            term = dot_nt(gq_ref[c], rows_of(w_ref.at[c], block, width))
            part = term if part is None else part + term
        unit = (by_rel[rel][...].astype(F32) - mean) * inverse
        plain = plain + jnp.sum(part, axis=-1, keepdims=True)
        weighted = weighted + jnp.sum(part * unit, axis=-1, keepdims=True)
        ref = out_by_rel[rel]
        ref[:, :width] = part.astype(ref.dtype)
    stat_ref[:, 0:1] = plain
    stat_ref[:, 1:2] = weighted
    lane = lax.broadcasted_iota(jnp.int32, (plain.shape[0], 128), 1)
    plain_high, weighted_high = plain.astype(BF16).astype(F32), weighted.astype(BF16).astype(F32)
    packed = jnp.where(lane == 0, plain_high, jnp.where(lane == 1, plain - plain_high, 0.0))
    packed = jnp.where(lane == 2, weighted_high, jnp.where(lane == 3, weighted - weighted_high, packed))
    for ref in norm_refs[1:]:
        ref[:, width:] = packed.astype(BF16)


def middle_kernel(info, *refs):
    x_refs, grad_ref, w_ref = refs[:4], refs[4], refs[5]
    normed_ref, qkv_ref, attend_ref, context_ref, moment_ref, stat_ref = refs[6:12]
    norm_refs, gq_ref = refs[12:16], refs[16]
    mean, inverse = row_moments(x_refs)
    moment_ref[:, 0:1] = mean
    moment_ref[:, 1:2] = inverse
    queries, keys, values = project(info, x_refs, w_ref, mean, inverse, normed_ref)
    qkv_ref[0] = queries
    qkv_ref[1] = keys
    qkv_ref[2] = values
    for head, cols in enumerate(head_slices(queries.shape[1])):
        attend, context = attend_head(info, queries[:, cols], keys[:, cols], values[:, cols])
        attend_ref[head] = attend
        context_ref[:, cols] = context
    attend_backward(qkv_ref, attend_ref, grad_ref[...], gq_ref)
    norm_parts(info, x_refs, mean, inverse, gq_ref, w_ref, stat_ref, norm_refs)


def norm_kernel(info, *refs):
    x_refs, moment_ref, gq_ref, w_ref = refs[:4], refs[4], refs[5], refs[6]
    stat_ref, norm_refs = refs[7], refs[8:12]
    mean, inverse = moment_ref[:, 0:1], moment_ref[:, 1:2]
    norm_parts(info, x_refs, mean, inverse, gq_ref, w_ref, stat_ref, norm_refs)


def last_kernel(info, *refs):
    g_refs, w_ref, qkv_ref, attend_ref, normed_ref, context_ref = refs[:4], *refs[4:9]
    gq_ref, outs = refs[9], refs[10:18]
    masked_ref, block_ref = refs[18:20]
    grad = context_grad(info, g_refs, w_ref, masked_ref)
    attend_backward(qkv_ref, attend_ref, grad, gq_ref)
    rows = outs[0].shape[-2]
    for c in range(4):
        for z in range(4):
            left = normed_ref[z] if c < 3 else masked_ref[z]
            right = gq_ref[c] if c < 3 else context_ref[...]
            block_ref[c, pl.ds(z * left.shape[1], left.shape[1]), :] = dot_tn(left, right).astype(BF16)
    for side in range(2):
        core = info[3] if side == 0 else 1 - info[3]
        for far, rel_far in enumerate(REL_PUT):
            for near, rel_near in enumerate(REL_PUT):
                place = pl.ds(place_row(info, rel_near, rel_far, core, rows), rows)
                for c in range(4):
                    outs[side * 4 + far][near, c] = block_ref[c, place, :]


VMEM = pl.BlockSpec(memory_space=pltpu.VMEM)
SMEM = pl.BlockSpec(memory_space=pltpu.SMEM)
ANY = pl.BlockSpec(memory_space=pl.ANY)


def call(kernel, outs, in_specs, scratch, flops, args, megabytes, out_specs=None):
    moved = sum(a.size * a.dtype.itemsize for a in args)
    return pl.pallas_call(
        kernel,
        out_shape=outs,
        in_specs=in_specs,
        out_specs=out_specs or [VMEM] * len(outs),
        scratch_shapes=scratch,
        compiler_params=pltpu.CompilerParams(vmem_limit_bytes=megabytes << 20),
        cost_estimate=pl.CostEstimate(flops=flops, bytes_accessed=moved, transcendentals=0),
    )(*args)


def shape(dims, dtype=BF16):
    return jax.ShapeDtypeStruct(dims, dtype)


def local(frames, lengths, qkv_weight, out_weight, grad_out):
    rows, own_width = frames.shape
    shard_rows, heads_width = qkv_weight.shape[2:]
    heads = heads_width // HEAD
    width = own_width * lax.axis_size("tensor")
    place = lax.axis_index("fsdp")
    section = lax.axis_index("section")
    on_first = section == 0
    info = jnp.stack(
        [lax.axis_index("tensor"), place // 8, place // 2 % 4, place % 2, section, lengths[0]]
    ).astype(jnp.int32)
    live_rows = (jnp.arange(rows, dtype=jnp.int32)[:, None] < lengths[0]).astype(F32)

    shard = jnp.concatenate([qkv_weight[0], out_weight[0].T[None]], 0)
    w_parts, x_first, g_first, ready = gather_weights(shard, frames, grad_out)

    block = (rows, own_width)
    wide = (rows, own_width + 128)
    wq_dims, wo_dims = (3, width, heads_width), (width, heads_width)
    project_flops = 2 * rows * width * 3 * heads_width
    part_sems = pltpu.SemaphoreType.DMA((32,))
    piece_sems = pltpu.SemaphoreType.DMA((4,))
    mixed = call(
        first_kernel,
        [shape(block, F32), shape(block), shape(block), shape(block)],
        [SMEM] + [ANY] * 15,
        [
            pltpu.VMEM((4, *block), BF16),
            pltpu.VMEM(wq_dims, BF16),
            pltpu.VMEM(wo_dims, BF16),
            pltpu.VMEM((rows, heads_width), BF16),
            piece_sems,
            part_sems,
            part_sems,
        ],
        4 * project_flops // 3,
        (info, *x_first, *w_parts, ready),
        56,
    )

    def finish(x_own, moments, stats, parts, own_grad):
        opposite = shift_tensor(parts[3], 2)
        arrived = [shift_tensor(parts[1], 1), shift_tensor(parts[2], -1), opposite]
        norm_grad = parts[0]
        plain, weighted = stats[:, 0:1], stats[:, 1:2]
        for part in arrived:
            part = part.astype(F32)
            norm_grad = norm_grad + part[:, :own_width]
            sums = part[:, own_width : own_width + 4]
            plain = plain + (sums[:, 0:1] + sums[:, 1:2])
            weighted = weighted + (sums[:, 2:3] + sums[:, 3:4])
        mean, inverse = moments[:, 0:1], moments[:, 1:2]
        unit = (x_own.astype(F32) - mean) * inverse
        centered = norm_grad - plain / width - unit * (weighted / width)
        return (own_grad.astype(F32) + inverse * centered).astype(BF16)

    opposite = shift_tensor(mixed[3], 2)
    arrived = [shift_tensor(mixed[1], 1), shift_tensor(mixed[2], -1), opposite]
    mixed_own = mixed[0] + sum(part.astype(F32) for part in arrived)
    first_out = (frames.astype(F32) + live_rows * mixed_own).astype(BF16)
    grad_top, w_out, w_qkv = call(
        context_grad_kernel,
        [shape((rows, heads_width)), shape(wo_dims), shape(wq_dims)],
        [SMEM] + [ANY] * 14,
        [pltpu.VMEM((4, *block), BF16), piece_sems, part_sems, part_sems],
        project_flops // 3,
        (info, *g_first, *w_parts),
        56,
        [VMEM, VMEM, ANY],
    )
    first_out, grad_top = lax.optimization_barrier((first_out, grad_top))

    entry = jnp.where(on_first, frames, cross_section(first_out, 0))
    x_entry = gather_tensor(entry)
    (w_loaded,) = call(
        load_kernel,
        [shape(wq_dims)],
        [ANY],
        [pltpu.SemaphoreType.DMA(())],
        0,
        (lax.optimization_barrier((w_qkv, entry))[0],),
        8,
    )
    norm_outs = [shape((rows, 2), F32), shape(block, F32), shape(wide), shape(wide), shape(wide)]
    normed, qkv, attend, context, moments, stats, *parts = call(
        middle_kernel,
        [
            shape((4, *block)),
            shape((3, rows, heads_width)),
            shape((heads, rows, rows), F32),
            shape((rows, heads_width)),
            shape((rows, 2), F32),
        ]
        + norm_outs,
        [SMEM] + [VMEM] * 6,
        [pltpu.VMEM((3, rows, heads_width), BF16)],
        2 * project_flops,
        (info, *x_entry, grad_top, w_loaded),
        16,
    )
    upper_grad = finish(x_entry[0], moments, stats, parts, grad_out)
    top_grad = jnp.where(on_first, cross_section(upper_grad, 1), grad_out)
    gq, *blocks = call(
        last_kernel,
        [shape((3, rows, heads_width))] + [shape((4, 4, shard_rows, heads_width))] * 8,
        [SMEM] + [VMEM] * 9,
        [pltpu.VMEM((4, *block), BF16), pltpu.VMEM((4, *wo_dims), BF16)],
        2 * project_flops,
        (info, *gather_tensor(top_grad), w_out, qkv, attend, normed, context),
        28,
    )
    arrived = {i: swap_cores(blocks[4 + i]) for i in (3, 1, 2, 0)}
    gq, arrived[3] = lax.optimization_barrier((gq, arrived[3]))
    line = ring_put([add(blocks[i], arrived[i]) for i in range(4)], FAR)
    weight_grad = ring_put([line[i] for i in range(4)], NEAR)
    stats, *parts = call(
        norm_kernel,
        norm_outs,
        [SMEM] + [VMEM] * 7,
        [],
        project_flops,
        (info, *x_entry, moments, gq, w_qkv),
        16,
    )
    grad_in = finish(x_entry[0], moments, stats, parts, top_grad)
    return (grad_in[None], weight_grad[None, :3], weight_grad[3].T[None])


def solution(mesh):
    in_specs = (
        P("fsdp", "tensor"),
        P("fsdp"),
        P("section", None, "fsdp", "tensor"),
        P("section", "tensor", "fsdp"),
        P("fsdp", "tensor"),
    )
    out_specs = (
        P("section", "fsdp", "tensor"),
        P("section", None, "fsdp", "tensor"),
        P("section", "tensor", "fsdp"),
    )
    return jax.shard_map(local, mesh=mesh, in_specs=in_specs, out_specs=out_specs, check_vma=False)
```

```python
import jax
import jax.numpy as jnp
from jax import lax
from jax.experimental import pallas as pl
from jax.experimental.pallas import tpu as pltpu
from jax.sharding import PartitionSpec as P

HEAD = 128
EPSILON = 1e-05
F32 = jnp.float32
BF16 = jnp.bfloat16

REL_GET = (0, 3, 1, 2)
REL_PUT = (0, 1, 3, 2)

NEAR, FAR = "zy", "yz"


def shift_tensor(value, step):
    count = lax.axis_size("tensor")
    return lax.ppermute(value, "tensor", [(i, (i + step) % count) for i in range(count)])


def cross_section(value, source):
    return lax.ppermute(value, "section", [(source, 1 - source)])


def shift_grid(value, axes, step):
    pairs = []
    for section in range(2):
        for z in range(4):
            for y in range(4):
                for core in range(2):
                    to_z, to_y = ((z + step) % 4, y) if axes[section] == "z" else (z, (y + step) % 4)
                    pairs.append(
                        (section * 32 + z * 8 + y * 2 + core, section * 32 + to_z * 8 + to_y * 2 + core)
                    )
    return lax.ppermute(value, ("section", "fsdp"), pairs)


def swap_cores(value):
    count = lax.axis_size("fsdp")
    return lax.ppermute(value, "fsdp", [(i, i ^ 1) for i in range(count)])


def gather_tensor(own):
    opposite = shift_tensor(own, 2)
    return (own, shift_tensor(own, 1), shift_tensor(own, -1), opposite)


def gather_weights(shard, x_own, g_own):
    opposite = shift_grid(shard, NEAR, 2)
    behind, ahead = shift_grid(shard, NEAR, 1), shift_grid(shard, NEAR, -1)
    x_pieces = gather_tensor(x_own)
    opposite, behind, ahead, x_pieces = lax.optimization_barrier((opposite, behind, ahead, x_pieces))
    ready = cross_section(opposite[0, :16, :128], 0)
    line = jnp.stack([shard, behind, ahead, opposite])
    line, ready, g_own = lax.optimization_barrier((line, ready, g_own))
    behind, ahead = shift_grid(line, FAR, 1), shift_grid(line, FAR, -1)
    g_pieces = gather_tensor(g_own)
    behind, ahead, g_pieces = lax.optimization_barrier((behind, ahead, g_pieces))
    low, high = shift_grid(behind[:2], FAR, 1), shift_grid(ahead[2:], FAR, -1)
    mine = (line, behind, ahead, low, high)
    return mine + tuple(swap_cores(part) for part in mine), x_pieces, g_pieces, ready


def add(*terms):
    total = terms[0].astype(F32)
    for term in terms[1:]:
        total = total + term.astype(F32)
    return total.astype(BF16)


def ring_put(blocks, axes):
    own, ahead, behind, opposite = blocks
    half = own.shape[0] // 2
    low, high = shift_grid(opposite[:half], axes, 1), shift_grid(opposite[half:], axes, -1)
    ahead = jnp.concatenate([add(ahead[:half], low), ahead[half:]], 0)
    behind = jnp.concatenate([behind[:half], add(behind[half:], high)], 0)
    return add(own, shift_grid(ahead, axes, 1), shift_grid(behind, axes, -1))


def dot_nn(a, b):
    return jnp.dot(a, b, preferred_element_type=F32)


def dot_nt(a, b):
    return lax.dot_general(a, b, (((1,), (1,)), ((), ())), preferred_element_type=F32)


def dot_tn(a, b):
    return lax.dot_general(a, b, (((0,), (0,)), ((), ())), preferred_element_type=F32)


def block_of(info, rel):
    return lax.rem(info[0] + rel, 4)


def rows_of(ref, block, width):
    return ref[pl.ds(pl.multiple_of(block * width, width), width), :]


def live_column(info, rows):
    return lax.broadcasted_iota(jnp.int32, (rows, 1), 0) < info[5]


def row_moments(x_refs):
    width = sum(ref.shape[1] for ref in x_refs)
    total = sum(jnp.sum(ref[...].astype(F32), axis=-1, keepdims=True) for ref in x_refs)
    mean = total / width
    square = 0.0
    for ref in x_refs:
        centered = ref[...].astype(F32) - mean
        square = square + jnp.sum(centered * centered, axis=-1, keepdims=True)
    return mean, lax.rsqrt(square / width + EPSILON)


def project(info, x_refs, w_ref, mean, inverse, normed_ref=None):
    totals = [None, None, None]
    for rel, ref in zip(REL_GET, x_refs):
        block = block_of(info, rel)
        normed = ((ref[...].astype(F32) - mean) * inverse).astype(BF16)
        if normed_ref is not None:
            normed_ref[block] = normed
        for c in range(3):
            part = dot_nn(normed, rows_of(w_ref.at[c], block, ref.shape[1]))
            totals[c] = part if totals[c] is None else totals[c] + part
    return [total.astype(BF16) for total in totals]


def attend_head(info, queries, keys, values):
    rows = queries.shape[0]
    scores = dot_nt(queries, keys) * (float(HEAD) ** -0.5)
    live_keys = lax.broadcasted_iota(jnp.int32, (rows, rows), 1) < info[5]
    scores = jnp.where(live_keys, scores, F32(-1e30))
    raised = jnp.exp(scores - jnp.max(scores, axis=-1, keepdims=True))
    attend = raised / jnp.sum(raised, axis=-1, keepdims=True)
    return attend, dot_nn(attend.astype(BF16), values).astype(BF16)


def head_slices(width):
    return [slice(start, start + HEAD) for start in range(0, width, HEAD)]


def place_row(info, rel_near, rel_far, core, rows):
    rel_z = lax.select(info[4] == 0, rel_near, rel_far)
    rel_y = lax.select(info[4] == 0, rel_far, rel_near)
    z, y = lax.rem(info[1] + rel_z, 4), lax.rem(info[2] + rel_y, 4)
    return pl.multiple_of(((z * 4 + y) * 2 + core) * rows, rows)


def start_all(sources, target_ref, sems):
    copies = [pltpu.make_async_copy(ref, target_ref.at[i], sems.at[i]) for i, ref in enumerate(sources)]
    for copy in copies:
        copy.start()
    return copies


def part_copies(info, parts, matrices, target_ref, sems):
    copies = []
    rows = parts[0].shape[-2]
    for side in range(2):
        core = info[3] if side == 0 else 1 - info[3]
        for far, rel_far in enumerate(REL_GET):
            for near, rel_near in enumerate(REL_GET):
                array = parts[side * 5 + (far if far < 3 else 3 + near // 2)]
                source = array.at[near if far < 3 else near % 2, matrices]
                place = pl.ds(place_row(info, rel_near, rel_far, core, rows), rows)
                target = target_ref.at[:, place, :] if isinstance(matrices, pl.Slice) else target_ref.at[place, :]
                copies.append(pltpu.make_async_copy(source, target, sems.at[len(copies)]))
    for copy in copies:
        copy.start()
    return copies


def first_kernel(info, *refs):
    x_sources, parts = refs[:4], refs[4:14]
    mixed_refs = refs[15:19]
    x_ref, wq_ref, wo_ref, context_ref, x_sems, q_sems, o_sems = refs[19:]
    x_copies = start_all(x_sources, x_ref, x_sems)
    x_refs = [x_ref.at[i] for i in range(4)]
    q_copies = part_copies(info, parts, pl.ds(0, 3), wq_ref, q_sems)
    o_copies = part_copies(info, parts, 3, wo_ref, o_sems)
    for copy in x_copies:
        copy.wait()
    mean, inverse = row_moments(x_refs)
    for copy in q_copies:
        copy.wait()
    queries, keys, values = project(info, x_refs, wq_ref, mean, inverse)
    for cols in head_slices(queries.shape[1]):
        _, context_ref[:, cols] = attend_head(info, queries[:, cols], keys[:, cols], values[:, cols])
    context = context_ref[...]
    for copy in o_copies:
        copy.wait()
    for rel, ref in zip(REL_PUT, mixed_refs):
        ref[...] = dot_nt(context, rows_of(wo_ref, block_of(info, rel), ref.shape[1])).astype(ref.dtype)


def load_kernel(source_ref, target_ref, sem):
    copy = pltpu.make_async_copy(source_ref, target_ref, sem)
    copy.start()
    copy.wait()


def context_grad(info, g_refs, w_ref, masked_ref=None):
    live = live_column(info, g_refs[0].shape[0])
    total = None
    for rel, ref in zip(REL_GET, g_refs):
        block = block_of(info, rel)
        masked = jnp.where(live, ref[...].astype(F32), 0.0).astype(BF16)
        if masked_ref is not None:
            masked_ref[block] = masked
        part = dot_nn(masked, rows_of(w_ref, block, ref.shape[1]))
        total = part if total is None else total + part
    return total.astype(BF16)


def context_grad_kernel(info, *refs):
    g_sources, parts, grad_ref, w_ref, wq_out = refs[:4], refs[4:14], *refs[14:17]
    g_ref, wq_ref, g_sems, w_sems, q_sems, out_sem = refs[17:]
    q_copies = part_copies(info, parts, pl.ds(0, 3), wq_ref, q_sems)
    copies = start_all(g_sources, g_ref, g_sems) + part_copies(info, parts, 3, w_ref, w_sems)
    for copy in q_copies:
        copy.wait()
    save = pltpu.make_async_copy(wq_ref, wq_out, out_sem)
    save.start()
    for copy in copies:
        copy.wait()
    grad_ref[...] = context_grad(info, [g_ref.at[i] for i in range(4)], w_ref)
    save.wait()


def attend_backward(qkv_ref, attend_ref, grad, gq_ref):
    scale = float(HEAD) ** -0.5
    for head, cols in enumerate(head_slices(grad.shape[1])):
        grad_head = grad[:, cols]
        queries, keys, values = (qkv_ref[c, :, cols] for c in range(3))
        attend = attend_ref[head]
        grad_attend = dot_nt(grad_head, values)
        gq_ref[2, :, cols] = dot_tn(attend.astype(BF16), grad_head).astype(BF16)
        inner = jnp.sum(grad_attend * attend, axis=-1, keepdims=True)
        grad_scores = (attend * (grad_attend - inner) * scale).astype(BF16)
        gq_ref[0, :, cols] = dot_nn(grad_scores, keys).astype(BF16)
        gq_ref[1, :, cols] = dot_tn(grad_scores, queries).astype(BF16)


def norm_parts(info, x_refs, mean, inverse, gq_ref, w_ref, stat_ref, norm_refs):
    width = x_refs[0].shape[1]
    plain, weighted = 0.0, 0.0
    by_rel = dict(zip(REL_GET, x_refs))
    out_by_rel = dict(zip(REL_PUT, norm_refs))
    for rel in REL_PUT:
        block = block_of(info, rel)
        part = None
        for c in range(3):
            term = dot_nt(gq_ref[c], rows_of(w_ref.at[c], block, width))
            part = term if part is None else part + term
        unit = (by_rel[rel][...].astype(F32) - mean) * inverse
        plain = plain + jnp.sum(part, axis=-1, keepdims=True)
        weighted = weighted + jnp.sum(part * unit, axis=-1, keepdims=True)
        ref = out_by_rel[rel]
        ref[:, :width] = part.astype(ref.dtype)
    stat_ref[:, 0:1] = plain
    stat_ref[:, 1:2] = weighted
    lane = lax.broadcasted_iota(jnp.int32, (plain.shape[0], 128), 1)
    plain_high, weighted_high = plain.astype(BF16).astype(F32), weighted.astype(BF16).astype(F32)
    packed = jnp.where(lane == 0, plain_high, jnp.where(lane == 1, plain - plain_high, 0.0))
    packed = jnp.where(lane == 2, weighted_high, jnp.where(lane == 3, weighted - weighted_high, packed))
    for ref in norm_refs[1:]:
        ref[:, width:] = packed.astype(BF16)


def middle_kernel(info, *refs):
    x_refs, grad_ref, w_ref = refs[:4], refs[4], refs[5]
    normed_ref, qkv_ref, attend_ref, context_ref, moment_ref, stat_ref = refs[6:12]
    norm_refs, gq_ref = refs[12:16], refs[16]
    mean, inverse = row_moments(x_refs)
    moment_ref[:, 0:1] = mean
    moment_ref[:, 1:2] = inverse
    queries, keys, values = project(info, x_refs, w_ref, mean, inverse, normed_ref)
    qkv_ref[0] = queries
    qkv_ref[1] = keys
    qkv_ref[2] = values
    for head, cols in enumerate(head_slices(queries.shape[1])):
        attend, context = attend_head(info, queries[:, cols], keys[:, cols], values[:, cols])
        attend_ref[head] = attend
        context_ref[:, cols] = context
    attend_backward(qkv_ref, attend_ref, grad_ref[...], gq_ref)
    norm_parts(info, x_refs, mean, inverse, gq_ref, w_ref, stat_ref, norm_refs)


def norm_kernel(info, *refs):
    x_refs, moment_ref, gq_ref, w_ref = refs[:4], refs[4], refs[5], refs[6]
    stat_ref, norm_refs = refs[7], refs[8:12]
    mean, inverse = moment_ref[:, 0:1], moment_ref[:, 1:2]
    norm_parts(info, x_refs, mean, inverse, gq_ref, w_ref, stat_ref, norm_refs)


def last_kernel(info, *refs):
    g_refs, w_ref, qkv_ref, attend_ref, normed_ref, context_ref = refs[:4], *refs[4:9]
    gq_ref, outs = refs[9], refs[10:18]
    masked_ref, block_ref = refs[18:20]
    grad = context_grad(info, g_refs, w_ref, masked_ref)
    attend_backward(qkv_ref, attend_ref, grad, gq_ref)
    rows = outs[0].shape[-2]
    for c in range(4):
        for z in range(4):
            left = normed_ref[z] if c < 3 else masked_ref[z]
            right = gq_ref[c] if c < 3 else context_ref[...]
            block_ref[c, pl.ds(z * left.shape[1], left.shape[1]), :] = dot_tn(left, right).astype(BF16)
    for side in range(2):
        core = info[3] if side == 0 else 1 - info[3]
        for far, rel_far in enumerate(REL_PUT):
            for near, rel_near in enumerate(REL_PUT):
                place = pl.ds(place_row(info, rel_near, rel_far, core, rows), rows)
                for c in range(4):
                    outs[side * 4 + far][near, c] = block_ref[c, place, :]


VMEM = pl.BlockSpec(memory_space=pltpu.VMEM)
SMEM = pl.BlockSpec(memory_space=pltpu.SMEM)
ANY = pl.BlockSpec(memory_space=pl.ANY)


def call(kernel, outs, in_specs, scratch, flops, args, megabytes, out_specs=None):
    moved = sum(a.size * a.dtype.itemsize for a in args)
    return pl.pallas_call(
        kernel,
        out_shape=outs,
        in_specs=in_specs,
        out_specs=out_specs or [VMEM] * len(outs),
        scratch_shapes=scratch,
        compiler_params=pltpu.CompilerParams(vmem_limit_bytes=megabytes << 20),
        cost_estimate=pl.CostEstimate(flops=flops, bytes_accessed=moved, transcendentals=0),
    )(*args)


def shape(dims, dtype=BF16):
    return jax.ShapeDtypeStruct(dims, dtype)


def local(frames, lengths, qkv_weight, out_weight, grad_out):
    rows, own_width = frames.shape
    shard_rows, heads_width = qkv_weight.shape[2:]
    heads = heads_width // HEAD
    width = own_width * lax.axis_size("tensor")
    place = lax.axis_index("fsdp")
    section = lax.axis_index("section")
    on_first = section == 0
    info = jnp.stack(
        [lax.axis_index("tensor"), place // 8, place // 2 % 4, place % 2, section, lengths[0]]
    ).astype(jnp.int32)
    live_rows = (jnp.arange(rows, dtype=jnp.int32)[:, None] < lengths[0]).astype(F32)

    shard = jnp.concatenate([qkv_weight[0], out_weight[0].T[None]], 0)
    w_parts, x_first, g_first, ready = gather_weights(shard, frames, grad_out)

    block = (rows, own_width)
    wide = (rows, own_width + 128)
    wq_dims, wo_dims = (3, width, heads_width), (width, heads_width)
    project_flops = 2 * rows * width * 3 * heads_width
    part_sems = pltpu.SemaphoreType.DMA((32,))
    piece_sems = pltpu.SemaphoreType.DMA((4,))
    mixed = call(
        first_kernel,
        [shape(block, F32), shape(block), shape(block), shape(block)],
        [SMEM] + [ANY] * 15,
        [
            pltpu.VMEM((4, *block), BF16),
            pltpu.VMEM(wq_dims, BF16),
            pltpu.VMEM(wo_dims, BF16),
            pltpu.VMEM((rows, heads_width), BF16),
            piece_sems,
            part_sems,
            part_sems,
        ],
        4 * project_flops // 3,
        (info, *x_first, *w_parts, ready),
        56,
    )

    def finish(x_own, moments, stats, parts, own_grad):
        opposite = shift_tensor(parts[3], 2)
        arrived = [shift_tensor(parts[1], 1), shift_tensor(parts[2], -1), opposite]
        norm_grad = parts[0]
        plain, weighted = stats[:, 0:1], stats[:, 1:2]
        for part in arrived:
            part = part.astype(F32)
            norm_grad = norm_grad + part[:, :own_width]
            sums = part[:, own_width : own_width + 4]
            plain = plain + (sums[:, 0:1] + sums[:, 1:2])
            weighted = weighted + (sums[:, 2:3] + sums[:, 3:4])
        mean, inverse = moments[:, 0:1], moments[:, 1:2]
        unit = (x_own.astype(F32) - mean) * inverse
        centered = norm_grad - plain / width - unit * (weighted / width)
        return (own_grad.astype(F32) + inverse * centered).astype(BF16)

    opposite = shift_tensor(mixed[3], 2)
    arrived = [shift_tensor(mixed[1], 1), shift_tensor(mixed[2], -1), opposite]
    mixed_own = mixed[0] + sum(part.astype(F32) for part in arrived)
    first_out = (frames.astype(F32) + live_rows * mixed_own).astype(BF16)
    grad_top, w_out, w_qkv = call(
        context_grad_kernel,
        [shape((rows, heads_width)), shape(wo_dims), shape(wq_dims)],
        [SMEM] + [ANY] * 14,
        [
            pltpu.VMEM((4, *block), BF16),
            pltpu.VMEM(wq_dims, BF16),
            piece_sems,
            part_sems,
            part_sems,
            pltpu.SemaphoreType.DMA(()),
        ],
        project_flops // 3,
        (info, *g_first, *w_parts),
        56,
        [VMEM, VMEM, ANY],
    )
    first_out, grad_top = lax.optimization_barrier((first_out, grad_top))

    entry = jnp.where(on_first, frames, cross_section(first_out, 0))
    x_entry = gather_tensor(entry)
    (w_loaded,) = call(
        load_kernel,
        [shape(wq_dims)],
        [ANY],
        [pltpu.SemaphoreType.DMA(())],
        0,
        (lax.optimization_barrier((w_qkv, entry))[0],),
        8,
    )
    norm_outs = [shape((rows, 2), F32), shape(block, F32), shape(wide), shape(wide), shape(wide)]
    normed, qkv, attend, context, moments, stats, *parts = call(
        middle_kernel,
        [
            shape((4, *block)),
            shape((3, rows, heads_width)),
            shape((heads, rows, rows), F32),
            shape((rows, heads_width)),
            shape((rows, 2), F32),
        ]
        + norm_outs,
        [SMEM] + [VMEM] * 6,
        [pltpu.VMEM((3, rows, heads_width), BF16)],
        2 * project_flops,
        (info, *x_entry, grad_top, w_loaded),
        16,
    )
    upper_grad = finish(x_entry[0], moments, stats, parts, grad_out)
    top_grad = jnp.where(on_first, cross_section(upper_grad, 1), grad_out)
    gq, *blocks = call(
        last_kernel,
        [shape((3, rows, heads_width))] + [shape((4, 4, shard_rows, heads_width))] * 8,
        [SMEM] + [VMEM] * 9,
        [pltpu.VMEM((4, *block), BF16), pltpu.VMEM((4, *wo_dims), BF16)],
        2 * project_flops,
        (info, *gather_tensor(top_grad), w_out, qkv, attend, normed, context),
        28,
    )
    arrived = {i: swap_cores(blocks[4 + i]) for i in (3, 1, 2, 0)}
    gq, arrived[3] = lax.optimization_barrier((gq, arrived[3]))
    line = ring_put([add(blocks[i], arrived[i]) for i in range(4)], FAR)
    weight_grad = ring_put([line[i] for i in range(4)], NEAR)
    stats, *parts = call(
        norm_kernel,
        norm_outs,
        [SMEM] + [VMEM] * 7,
        [],
        project_flops,
        (info, *x_entry, moments, gq, w_qkv),
        16,
    )
    grad_in = finish(x_entry[0], moments, stats, parts, top_grad)
    return (grad_in[None], weight_grad[None, :3], weight_grad[3].T[None])


def solution(mesh):
    in_specs = (
        P("fsdp", "tensor"),
        P("fsdp"),
        P("section", None, "fsdp", "tensor"),
        P("section", "tensor", "fsdp"),
        P("fsdp", "tensor"),
    )
    out_specs = (
        P("section", "fsdp", "tensor"),
        P("section", None, "fsdp", "tensor"),
        P("section", "tensor", "fsdp"),
    )
    return jax.shard_map(local, mesh=mesh, in_specs=in_specs, out_specs=out_specs, check_vma=False)
```

```python
import jax
import jax.numpy as jnp
from jax import lax
from jax.experimental import pallas as pl
from jax.experimental.pallas import tpu as pltpu
from jax.sharding import PartitionSpec as P

HEAD = 128
EPSILON = 1e-05
F32 = jnp.float32
BF16 = jnp.bfloat16

REL_GET = (0, 3, 1, 2)
REL_PUT = (0, 1, 3, 2)

NEAR, FAR = "zy", "yz"


def shift_tensor(value, step):
    count = lax.axis_size("tensor")
    return lax.ppermute(value, "tensor", [(i, (i + step) % count) for i in range(count)])


def cross_section(value, source):
    return lax.ppermute(value, "section", [(source, 1 - source)])


def shift_grid(value, axes, step):
    pairs = []
    for section in range(2):
        for z in range(4):
            for y in range(4):
                for core in range(2):
                    to_z, to_y = ((z + step) % 4, y) if axes[section] == "z" else (z, (y + step) % 4)
                    pairs.append(
                        (section * 32 + z * 8 + y * 2 + core, section * 32 + to_z * 8 + to_y * 2 + core)
                    )
    return lax.ppermute(value, ("section", "fsdp"), pairs)


def swap_cores(value):
    count = lax.axis_size("fsdp")
    return lax.ppermute(value, "fsdp", [(i, i ^ 1) for i in range(count)])


def gather_tensor(own):
    opposite = shift_tensor(own, 2)
    return (own, shift_tensor(own, 1), shift_tensor(own, -1), opposite)


def gather_weights(shard, x_own, g_own):
    opposite = shift_grid(shard, NEAR, 2)
    behind, ahead = shift_grid(shard, NEAR, 1), shift_grid(shard, NEAR, -1)
    x_pieces = gather_tensor(x_own)
    opposite, behind, ahead, x_pieces = lax.optimization_barrier((opposite, behind, ahead, x_pieces))
    ready = cross_section(opposite[0, :16, :128], 0)
    line = jnp.stack([shard, behind, ahead, opposite])
    line, ready, g_own = lax.optimization_barrier((line, ready, g_own))
    behind, ahead = shift_grid(line, FAR, 1), shift_grid(line, FAR, -1)
    g_pieces = gather_tensor(g_own)
    behind, ahead, g_pieces = lax.optimization_barrier((behind, ahead, g_pieces))
    low, high = shift_grid(behind[:2], FAR, 1), shift_grid(ahead[2:], FAR, -1)
    mine = (line, behind, ahead, low, high)
    return mine + tuple(swap_cores(part) for part in mine), x_pieces, g_pieces, ready


def add(*terms):
    total = terms[0].astype(F32)
    for term in terms[1:]:
        total = total + term.astype(F32)
    return total.astype(BF16)


def ring_put(blocks, axes):
    own, ahead, behind, opposite = blocks
    half = own.shape[0] // 2
    low, high = shift_grid(opposite[:half], axes, 1), shift_grid(opposite[half:], axes, -1)
    ahead = jnp.concatenate([add(ahead[:half], low), ahead[half:]], 0)
    behind = jnp.concatenate([behind[:half], add(behind[half:], high)], 0)
    return add(own, shift_grid(ahead, axes, 1), shift_grid(behind, axes, -1))


def dot_nn(a, b):
    return jnp.dot(a, b, preferred_element_type=F32)


def dot_nt(a, b):
    return lax.dot_general(a, b, (((1,), (1,)), ((), ())), preferred_element_type=F32)


def dot_tn(a, b):
    return lax.dot_general(a, b, (((0,), (0,)), ((), ())), preferred_element_type=F32)


def block_of(info, rel):
    return lax.rem(info[0] + rel, 4)


def rows_of(ref, block, width):
    return ref[pl.ds(pl.multiple_of(block * width, width), width), :]


def live_column(info, rows):
    return lax.broadcasted_iota(jnp.int32, (rows, 1), 0) < info[5]


def row_moments(x_refs):
    width = sum(ref.shape[1] for ref in x_refs)
    total = sum(jnp.sum(ref[...].astype(F32), axis=-1, keepdims=True) for ref in x_refs)
    mean = total / width
    square = 0.0
    for ref in x_refs:
        centered = ref[...].astype(F32) - mean
        square = square + jnp.sum(centered * centered, axis=-1, keepdims=True)
    return mean, lax.rsqrt(square / width + EPSILON)


def project(info, x_refs, w_ref, mean, inverse, normed_ref=None):
    totals = [None, None, None]
    for rel, ref in zip(REL_GET, x_refs):
        block = block_of(info, rel)
        normed = ((ref[...].astype(F32) - mean) * inverse).astype(BF16)
        if normed_ref is not None:
            normed_ref[block] = normed
        for c in range(3):
            part = dot_nn(normed, rows_of(w_ref.at[c], block, ref.shape[1]))
            totals[c] = part if totals[c] is None else totals[c] + part
    return [total.astype(BF16) for total in totals]


def attend_head(info, queries, keys, values):
    rows = queries.shape[0]
    scores = dot_nt(queries, keys) * (float(HEAD) ** -0.5)
    live_keys = lax.broadcasted_iota(jnp.int32, (rows, rows), 1) < info[5]
    scores = jnp.where(live_keys, scores, F32(-1e30))
    raised = jnp.exp(scores - jnp.max(scores, axis=-1, keepdims=True))
    attend = raised / jnp.sum(raised, axis=-1, keepdims=True)
    return attend, dot_nn(attend.astype(BF16), values).astype(BF16)


def head_slices(width):
    return [slice(start, start + HEAD) for start in range(0, width, HEAD)]


def place_row(info, rel_near, rel_far, core, rows):
    rel_z = lax.select(info[4] == 0, rel_near, rel_far)
    rel_y = lax.select(info[4] == 0, rel_far, rel_near)
    z, y = lax.rem(info[1] + rel_z, 4), lax.rem(info[2] + rel_y, 4)
    return pl.multiple_of(((z * 4 + y) * 2 + core) * rows, rows)


def start_all(sources, target_ref, sems):
    copies = [pltpu.make_async_copy(ref, target_ref.at[i], sems.at[i]) for i, ref in enumerate(sources)]
    for copy in copies:
        copy.start()
    return copies


def part_copies(info, parts, matrices, target_ref, sems):
    copies = []
    rows = parts[0].shape[-2]
    for side in range(2):
        core = info[3] if side == 0 else 1 - info[3]
        for far, rel_far in enumerate(REL_GET):
            for near, rel_near in enumerate(REL_GET):
                array = parts[side * 5 + (far if far < 3 else 3 + near // 2)]
                source = array.at[near if far < 3 else near % 2, matrices]
                place = pl.ds(place_row(info, rel_near, rel_far, core, rows), rows)
                target = target_ref.at[:, place, :] if isinstance(matrices, pl.Slice) else target_ref.at[place, :]
                copies.append(pltpu.make_async_copy(source, target, sems.at[len(copies)]))
    for copy in copies:
        copy.start()
    return copies


def first_kernel(info, *refs):
    x_sources, parts = refs[:4], refs[4:14]
    mixed_refs = refs[15:19]
    x_ref, wq_ref, wo_ref, context_ref, x_sems, q_sems, o_sems = refs[19:]

    @pl.when(info[4] == 0)
    def _():
        x_copies = start_all(x_sources, x_ref, x_sems)
        x_refs = [x_ref.at[i] for i in range(4)]
        q_copies = part_copies(info, parts, pl.ds(0, 3), wq_ref, q_sems)
        o_copies = part_copies(info, parts, 3, wo_ref, o_sems)
        for copy in x_copies:
            copy.wait()
        mean, inverse = row_moments(x_refs)
        for copy in q_copies:
            copy.wait()
        queries, keys, values = project(info, x_refs, wq_ref, mean, inverse)
        for cols in head_slices(queries.shape[1]):
            _, context_ref[:, cols] = attend_head(info, queries[:, cols], keys[:, cols], values[:, cols])
        context = context_ref[...]
        for copy in o_copies:
            copy.wait()
        for rel, ref in zip(REL_PUT, mixed_refs):
            terms = dot_nt(context, rows_of(wo_ref, block_of(info, rel), ref.shape[1]))
            ref[...] = terms.astype(ref.dtype)

    @pl.when(info[4] != 0)
    def _():
        for ref in mixed_refs:
            ref[...] = jnp.zeros_like(ref)


def load_kernel(source_ref, target_ref, sem):
    copy = pltpu.make_async_copy(source_ref, target_ref, sem)
    copy.start()
    copy.wait()


def context_grad(info, g_refs, w_ref, masked_ref=None):
    live = live_column(info, g_refs[0].shape[0])
    total = None
    for rel, ref in zip(REL_GET, g_refs):
        block = block_of(info, rel)
        masked = jnp.where(live, ref[...].astype(F32), 0.0).astype(BF16)
        if masked_ref is not None:
            masked_ref[block] = masked
        part = dot_nn(masked, rows_of(w_ref, block, ref.shape[1]))
        total = part if total is None else total + part
    return total.astype(BF16)


def context_grad_kernel(info, *refs):
    g_sources, parts, grad_ref, w_ref, wq_out = refs[:4], refs[4:14], *refs[14:17]
    g_ref, wq_ref, g_sems, w_sems, q_sems, out_sem = refs[17:]
    q_copies = part_copies(info, parts, pl.ds(0, 3), wq_ref, q_sems)
    w_copies = part_copies(info, parts, 3, w_ref, w_sems)
    for copy in q_copies:
        copy.wait()
    save = pltpu.make_async_copy(wq_ref, wq_out, out_sem)
    save.start()
    for copy in w_copies:
        copy.wait()

    @pl.when(info[4] == 1)
    def _():
        for copy in start_all(g_sources, g_ref, g_sems):
            copy.wait()
        grad_ref[...] = context_grad(info, [g_ref.at[i] for i in range(4)], w_ref)

    @pl.when(info[4] != 1)
    def _():
        grad_ref[...] = jnp.zeros_like(grad_ref)

    save.wait()


def attend_backward(qkv_ref, attend_ref, grad, gq_ref):
    scale = float(HEAD) ** -0.5
    for head, cols in enumerate(head_slices(grad.shape[1])):
        grad_head = grad[:, cols]
        queries, keys, values = (qkv_ref[c, :, cols] for c in range(3))
        attend = attend_ref[head]
        grad_attend = dot_nt(grad_head, values)
        gq_ref[2, :, cols] = dot_tn(attend.astype(BF16), grad_head).astype(BF16)
        inner = jnp.sum(grad_attend * attend, axis=-1, keepdims=True)
        grad_scores = (attend * (grad_attend - inner) * scale).astype(BF16)
        gq_ref[0, :, cols] = dot_nn(grad_scores, keys).astype(BF16)
        gq_ref[1, :, cols] = dot_tn(grad_scores, queries).astype(BF16)


def norm_parts(info, x_refs, mean, inverse, gq_ref, w_ref, stat_ref, norm_refs):
    width = x_refs[0].shape[1]
    plain, weighted = 0.0, 0.0
    by_rel = dict(zip(REL_GET, x_refs))
    out_by_rel = dict(zip(REL_PUT, norm_refs))
    for rel in REL_PUT:
        block = block_of(info, rel)
        part = None
        for c in range(3):
            term = dot_nt(gq_ref[c], rows_of(w_ref.at[c], block, width))
            part = term if part is None else part + term
        unit = (by_rel[rel][...].astype(F32) - mean) * inverse
        plain = plain + jnp.sum(part, axis=-1, keepdims=True)
        weighted = weighted + jnp.sum(part * unit, axis=-1, keepdims=True)
        ref = out_by_rel[rel]
        ref[:, :width] = part.astype(ref.dtype)
    stat_ref[:, 0:1] = plain
    stat_ref[:, 1:2] = weighted
    lane = lax.broadcasted_iota(jnp.int32, (plain.shape[0], 128), 1)
    plain_high, weighted_high = plain.astype(BF16).astype(F32), weighted.astype(BF16).astype(F32)
    packed = jnp.where(lane == 0, plain_high, jnp.where(lane == 1, plain - plain_high, 0.0))
    packed = jnp.where(lane == 2, weighted_high, jnp.where(lane == 3, weighted - weighted_high, packed))
    for ref in norm_refs[1:]:
        ref[:, width:] = packed.astype(BF16)


def middle_kernel(info, *refs):
    x_refs, grad_ref, w_ref = refs[:4], refs[4], refs[5]
    normed_ref, qkv_ref, attend_ref, context_ref, moment_ref, stat_ref = refs[6:12]
    norm_refs, gq_ref = refs[12:16], refs[16]
    mean, inverse = row_moments(x_refs)
    moment_ref[:, 0:1] = mean
    moment_ref[:, 1:2] = inverse
    queries, keys, values = project(info, x_refs, w_ref, mean, inverse, normed_ref)
    qkv_ref[0] = queries
    qkv_ref[1] = keys
    qkv_ref[2] = values
    for head, cols in enumerate(head_slices(queries.shape[1])):
        attend, context = attend_head(info, queries[:, cols], keys[:, cols], values[:, cols])
        attend_ref[head] = attend
        context_ref[:, cols] = context
    attend_backward(qkv_ref, attend_ref, grad_ref[...], gq_ref)
    norm_parts(info, x_refs, mean, inverse, gq_ref, w_ref, stat_ref, norm_refs)


def norm_kernel(info, *refs):
    x_refs, moment_ref, gq_ref, w_ref = refs[:4], refs[4], refs[5], refs[6]
    stat_ref, norm_refs = refs[7], refs[8:12]
    mean, inverse = moment_ref[:, 0:1], moment_ref[:, 1:2]
    norm_parts(info, x_refs, mean, inverse, gq_ref, w_ref, stat_ref, norm_refs)


def last_kernel(info, *refs):
    g_refs, w_ref, qkv_ref, attend_ref, normed_ref, context_ref = refs[:4], *refs[4:9]
    gq_ref, outs = refs[9], refs[10:18]
    masked_ref, block_ref = refs[18:20]
    grad = context_grad(info, g_refs, w_ref, masked_ref)
    attend_backward(qkv_ref, attend_ref, grad, gq_ref)
    rows = outs[0].shape[-2]
    for c in range(4):
        for z in range(4):
            left = normed_ref[z] if c < 3 else masked_ref[z]
            right = gq_ref[c] if c < 3 else context_ref[...]
            block_ref[c, pl.ds(z * left.shape[1], left.shape[1]), :] = dot_tn(left, right).astype(BF16)
    for side in range(2):
        core = info[3] if side == 0 else 1 - info[3]
        for far, rel_far in enumerate(REL_PUT):
            for near, rel_near in enumerate(REL_PUT):
                place = pl.ds(place_row(info, rel_near, rel_far, core, rows), rows)
                for c in range(4):
                    outs[side * 4 + far][near, c] = block_ref[c, place, :]


VMEM = pl.BlockSpec(memory_space=pltpu.VMEM)
SMEM = pl.BlockSpec(memory_space=pltpu.SMEM)
ANY = pl.BlockSpec(memory_space=pl.ANY)


def call(kernel, outs, in_specs, scratch, flops, args, megabytes, out_specs=None):
    moved = sum(a.size * a.dtype.itemsize for a in args)
    return pl.pallas_call(
        kernel,
        out_shape=outs,
        in_specs=in_specs,
        out_specs=out_specs or [VMEM] * len(outs),
        scratch_shapes=scratch,
        compiler_params=pltpu.CompilerParams(vmem_limit_bytes=megabytes << 20),
        cost_estimate=pl.CostEstimate(flops=flops, bytes_accessed=moved, transcendentals=0),
    )(*args)


def shape(dims, dtype=BF16):
    return jax.ShapeDtypeStruct(dims, dtype)


def local(frames, lengths, qkv_weight, out_weight, grad_out):
    rows, own_width = frames.shape
    shard_rows, heads_width = qkv_weight.shape[2:]
    heads = heads_width // HEAD
    width = own_width * lax.axis_size("tensor")
    place = lax.axis_index("fsdp")
    section = lax.axis_index("section")
    on_first = section == 0
    info = jnp.stack(
        [lax.axis_index("tensor"), place // 8, place // 2 % 4, place % 2, section, lengths[0]]
    ).astype(jnp.int32)
    live_rows = (jnp.arange(rows, dtype=jnp.int32)[:, None] < lengths[0]).astype(F32)

    shard = jnp.concatenate([qkv_weight[0], out_weight[0].T[None]], 0)
    w_parts, x_first, g_first, ready = gather_weights(shard, frames, grad_out)

    block = (rows, own_width)
    wide = (rows, own_width + 128)
    wq_dims, wo_dims = (3, width, heads_width), (width, heads_width)
    project_flops = 2 * rows * width * 3 * heads_width
    part_sems = pltpu.SemaphoreType.DMA((32,))
    piece_sems = pltpu.SemaphoreType.DMA((4,))
    mixed = call(
        first_kernel,
        [shape(block, F32), shape(block), shape(block), shape(block)],
        [SMEM] + [ANY] * 15,
        [
            pltpu.VMEM((4, *block), BF16),
            pltpu.VMEM(wq_dims, BF16),
            pltpu.VMEM(wo_dims, BF16),
            pltpu.VMEM((rows, heads_width), BF16),
            piece_sems,
            part_sems,
            part_sems,
        ],
        4 * project_flops // 3,
        (info, *x_first, *w_parts, ready),
        56,
    )

    def finish(x_own, moments, stats, parts, own_grad):
        opposite = shift_tensor(parts[3], 2)
        arrived = [shift_tensor(parts[1], 1), shift_tensor(parts[2], -1), opposite]
        norm_grad = parts[0]
        plain, weighted = stats[:, 0:1], stats[:, 1:2]
        for part in arrived:
            part = part.astype(F32)
            norm_grad = norm_grad + part[:, :own_width]
            sums = part[:, own_width : own_width + 4]
            plain = plain + (sums[:, 0:1] + sums[:, 1:2])
            weighted = weighted + (sums[:, 2:3] + sums[:, 3:4])
        mean, inverse = moments[:, 0:1], moments[:, 1:2]
        unit = (x_own.astype(F32) - mean) * inverse
        centered = norm_grad - plain / width - unit * (weighted / width)
        return (own_grad.astype(F32) + inverse * centered).astype(BF16)

    opposite = shift_tensor(mixed[3], 2)
    arrived = [shift_tensor(mixed[1], 1), shift_tensor(mixed[2], -1), opposite]
    mixed_own = mixed[0] + sum(part.astype(F32) for part in arrived)
    first_out = (frames.astype(F32) + live_rows * mixed_own).astype(BF16)
    grad_top, w_out, w_qkv = call(
        context_grad_kernel,
        [shape((rows, heads_width)), shape(wo_dims), shape(wq_dims)],
        [SMEM] + [ANY] * 14,
        [
            pltpu.VMEM((4, *block), BF16),
            pltpu.VMEM(wq_dims, BF16),
            piece_sems,
            part_sems,
            part_sems,
            pltpu.SemaphoreType.DMA(()),
        ],
        project_flops // 3,
        (info, *g_first, *w_parts),
        56,
        [VMEM, VMEM, ANY],
    )
    first_out, grad_top = lax.optimization_barrier((first_out, grad_top))

    entry = jnp.where(on_first, frames, cross_section(first_out, 0))
    x_entry = gather_tensor(entry)
    (w_loaded,) = call(
        load_kernel,
        [shape(wq_dims)],
        [ANY],
        [pltpu.SemaphoreType.DMA(())],
        0,
        (lax.optimization_barrier((w_qkv, entry))[0],),
        8,
    )
    norm_outs = [shape((rows, 2), F32), shape(block, F32), shape(wide), shape(wide), shape(wide)]
    normed, qkv, attend, context, moments, stats, *parts = call(
        middle_kernel,
        [
            shape((4, *block)),
            shape((3, rows, heads_width)),
            shape((heads, rows, rows), F32),
            shape((rows, heads_width)),
            shape((rows, 2), F32),
        ]
        + norm_outs,
        [SMEM] + [VMEM] * 6,
        [pltpu.VMEM((3, rows, heads_width), BF16)],
        2 * project_flops,
        (info, *x_entry, grad_top, w_loaded),
        16,
    )
    upper_grad = finish(x_entry[0], moments, stats, parts, grad_out)
    top_grad = jnp.where(on_first, cross_section(upper_grad, 1), grad_out)
    gq, *blocks = call(
        last_kernel,
        [shape((3, rows, heads_width))] + [shape((4, 4, shard_rows, heads_width))] * 8,
        [SMEM] + [VMEM] * 9,
        [pltpu.VMEM((4, *block), BF16), pltpu.VMEM((4, *wo_dims), BF16)],
        2 * project_flops,
        (info, *gather_tensor(top_grad), w_out, qkv, attend, normed, context),
        28,
    )
    arrived = {i: swap_cores(blocks[4 + i]) for i in (3, 1, 2, 0)}
    gq, arrived[3] = lax.optimization_barrier((gq, arrived[3]))
    line = ring_put([add(blocks[i], arrived[i]) for i in range(4)], FAR)
    weight_grad = ring_put([line[i] for i in range(4)], NEAR)
    stats, *parts = call(
        norm_kernel,
        norm_outs,
        [SMEM] + [VMEM] * 7,
        [],
        project_flops,
        (info, *x_entry, moments, gq, w_qkv),
        16,
    )
    grad_in = finish(x_entry[0], moments, stats, parts, top_grad)
    return (grad_in[None], weight_grad[None, :3], weight_grad[3].T[None])


def solution(mesh):
    in_specs = (
        P("fsdp", "tensor"),
        P("fsdp"),
        P("section", None, "fsdp", "tensor"),
        P("section", "tensor", "fsdp"),
        P("fsdp", "tensor"),
    )
    out_specs = (
        P("section", "fsdp", "tensor"),
        P("section", None, "fsdp", "tensor"),
        P("section", "tensor", "fsdp"),
    )
    return jax.shard_map(local, mesh=mesh, in_specs=in_specs, out_specs=out_specs, check_vma=False)
```

```python
import jax
import jax.numpy as jnp
from jax import lax
from jax.experimental import pallas as pl
from jax.experimental.pallas import tpu as pltpu
from jax.sharding import PartitionSpec as P

HEAD = 128
EPSILON = 1e-05
F32 = jnp.float32
BF16 = jnp.bfloat16

REL_GET = (0, 3, 1, 2)
REL_PUT = (0, 1, 3, 2)

NEAR, FAR = "zy", "yz"


def shift_tensor(value, step):
    count = lax.axis_size("tensor")
    return lax.ppermute(value, "tensor", [(i, (i + step) % count) for i in range(count)])


def cross_section(value, source):
    return lax.ppermute(value, "section", [(source, 1 - source)])


def shift_grid(value, axes, step):
    pairs = []
    for section in range(2):
        for z in range(4):
            for y in range(4):
                for core in range(2):
                    to_z, to_y = ((z + step) % 4, y) if axes[section] == "z" else (z, (y + step) % 4)
                    pairs.append(
                        (section * 32 + z * 8 + y * 2 + core, section * 32 + to_z * 8 + to_y * 2 + core)
                    )
    return lax.ppermute(value, ("section", "fsdp"), pairs)


def swap_cores(value):
    count = lax.axis_size("fsdp")
    return lax.ppermute(value, "fsdp", [(i, i ^ 1) for i in range(count)])


def gather_tensor(own):
    opposite = shift_tensor(own, 2)
    return (own, shift_tensor(own, 1), shift_tensor(own, -1), opposite)


def gather_weights(shard, x_own, g_own):
    opposite = shift_grid(shard, NEAR, 2)
    behind, ahead = shift_grid(shard, NEAR, 1), shift_grid(shard, NEAR, -1)
    x_pieces = gather_tensor(x_own)
    opposite, behind, ahead, x_pieces = lax.optimization_barrier((opposite, behind, ahead, x_pieces))
    ready = cross_section(opposite[0, :16, :128], 0)
    line = jnp.stack([shard, behind, ahead, opposite])
    line, ready, g_own = lax.optimization_barrier((line, ready, g_own))
    behind, ahead = shift_grid(line, FAR, 1), shift_grid(line, FAR, -1)
    g_pieces = gather_tensor(g_own)
    behind, ahead, g_pieces = lax.optimization_barrier((behind, ahead, g_pieces))
    low, high = shift_grid(behind[:2], FAR, 1), shift_grid(ahead[2:], FAR, -1)
    mine = (line, behind, ahead, low, high)
    return mine + tuple(swap_cores(part) for part in mine), x_pieces, g_pieces, ready


def add(*terms):
    total = terms[0].astype(F32)
    for term in terms[1:]:
        total = total + term.astype(F32)
    return total.astype(BF16)


def ring_put(blocks, axes):
    own, ahead, behind, opposite = blocks
    half = own.shape[0] // 2
    low, high = shift_grid(opposite[:half], axes, 1), shift_grid(opposite[half:], axes, -1)
    ahead = jnp.concatenate([add(ahead[:half], low), ahead[half:]], 0)
    behind = jnp.concatenate([behind[:half], add(behind[half:], high)], 0)
    return own, shift_grid(ahead, axes, 1), shift_grid(behind, axes, -1)


def dot_nn(a, b):
    return jnp.dot(a, b, preferred_element_type=F32)


def dot_nt(a, b):
    return lax.dot_general(a, b, (((1,), (1,)), ((), ())), preferred_element_type=F32)


def dot_tn(a, b):
    return lax.dot_general(a, b, (((0,), (0,)), ((), ())), preferred_element_type=F32)


def block_of(info, rel):
    return lax.rem(info[0] + rel, 4)


def rows_of(ref, block, width):
    return ref[pl.ds(pl.multiple_of(block * width, width), width), :]


def live_column(info, rows):
    return lax.broadcasted_iota(jnp.int32, (rows, 1), 0) < info[5]


def row_moments(x_refs):
    width = sum(ref.shape[1] for ref in x_refs)
    total = sum(jnp.sum(ref[...].astype(F32), axis=-1, keepdims=True) for ref in x_refs)
    mean = total / width
    square = 0.0
    for ref in x_refs:
        centered = ref[...].astype(F32) - mean
        square = square + jnp.sum(centered * centered, axis=-1, keepdims=True)
    return mean, lax.rsqrt(square / width + EPSILON)


def project(info, x_refs, w_ref, mean, inverse, normed_ref=None):
    totals = [None, None, None]
    for rel, ref in zip(REL_GET, x_refs):
        block = block_of(info, rel)
        normed = ((ref[...].astype(F32) - mean) * inverse).astype(BF16)
        if normed_ref is not None:
            normed_ref[block] = normed
        for c in range(3):
            part = dot_nn(normed, rows_of(w_ref.at[c], block, ref.shape[1]))
            totals[c] = part if totals[c] is None else totals[c] + part
    return [total.astype(BF16) for total in totals]


def attend_head(info, queries, keys, values):
    rows = queries.shape[0]
    scores = dot_nt(queries, keys) * (float(HEAD) ** -0.5)
    live_keys = lax.broadcasted_iota(jnp.int32, (rows, rows), 1) < info[5]
    scores = jnp.where(live_keys, scores, F32(-1e30))
    raised = jnp.exp(scores - jnp.max(scores, axis=-1, keepdims=True))
    attend = raised / jnp.sum(raised, axis=-1, keepdims=True)
    return attend, dot_nn(attend.astype(BF16), values).astype(BF16)


def head_slices(width):
    return [slice(start, start + HEAD) for start in range(0, width, HEAD)]


def place_row(info, rel_near, rel_far, core, rows):
    rel_z = lax.select(info[4] == 0, rel_near, rel_far)
    rel_y = lax.select(info[4] == 0, rel_far, rel_near)
    z, y = lax.rem(info[1] + rel_z, 4), lax.rem(info[2] + rel_y, 4)
    return pl.multiple_of(((z * 4 + y) * 2 + core) * rows, rows)


def start_all(sources, target_ref, sems):
    copies = [pltpu.make_async_copy(ref, target_ref.at[i], sems.at[i]) for i, ref in enumerate(sources)]
    for copy in copies:
        copy.start()
    return copies


def part_copies(info, parts, matrices, target_ref, sems, places=None):
    copies = []
    rows = parts[0].shape[-2]
    for side in range(2):
        core = info[3] if side == 0 else 1 - info[3]
        for far, rel_far in enumerate(REL_GET):
            for near, rel_near in enumerate(REL_GET):
                array = parts[side * 5 + (far if far < 3 else 3 + near // 2)]
                source = array.at[near if far < 3 else near % 2, matrices]
                place = pl.ds(place_row(info, rel_near, rel_far, core, rows), rows)
                target = target_ref.at[:, place, :] if isinstance(matrices, pl.Slice) else target_ref.at[place, :]
                copies.append(pltpu.make_async_copy(source, target, sems.at[len(copies)]))
                if places is not None:
                    places.append(place)
    for copy in copies:
        copy.start()
    return copies


def first_kernel(info, *refs):
    x_sources, parts = refs[:4], refs[4:14]
    mixed_refs = refs[15:19]
    x_ref, wq_ref, wo_ref, context_ref, x_sems, q_sems, o_sems = refs[19:]

    @pl.when(info[4] == 0)
    def _():
        x_copies = start_all([x_sources[REL_GET.index(rel)] for rel in range(4)], x_ref, x_sems)
        x_refs = [x_ref.at[rel] for rel in range(4)]
        q_copies = part_copies(info, parts, pl.ds(0, 3), wq_ref, q_sems)
        o_copies = part_copies(info, parts, 3, wo_ref, o_sems)
        for copy in x_copies:
            copy.wait()
        mean, inverse = row_moments(x_refs)
        totals = [None, None, None]
        for near, rel_near in enumerate(REL_GET):
            for copy in q_copies[near::4]:
                copy.wait()
            block = lax.rem(info[1] + rel_near, 4)
            piece = x_ref[lax.rem(block + 4 - info[0], 4)]
            normed = ((piece.astype(F32) - mean) * inverse).astype(BF16)
            for c in range(3):
                part = dot_nn(normed, rows_of(wq_ref.at[c], block, piece.shape[1]))
                totals[c] = part if totals[c] is None else totals[c] + part
        queries, keys, values = (total.astype(BF16) for total in totals)
        for cols in head_slices(queries.shape[1]):
            _, context_ref[:, cols] = attend_head(info, queries[:, cols], keys[:, cols], values[:, cols])
        context = context_ref[...]
        for copy in o_copies:
            copy.wait()
        for rel, ref in zip(REL_PUT, mixed_refs):
            terms = dot_nt(context, rows_of(wo_ref, block_of(info, rel), ref.shape[1]))
            ref[...] = terms.astype(ref.dtype)

    @pl.when(info[4] != 0)
    def _():
        for ref in mixed_refs:
            ref[...] = jnp.zeros_like(ref)


def load_kernel(source_ref, target_ref, sem):
    copy = pltpu.make_async_copy(source_ref, target_ref, sem)
    copy.start()
    copy.wait()


def context_grad(info, g_refs, w_ref, masked_ref=None):
    live = live_column(info, g_refs[0].shape[0])
    total = None
    for rel, ref in zip(REL_GET, g_refs):
        block = block_of(info, rel)
        masked = jnp.where(live, ref[...].astype(F32), 0.0).astype(BF16)
        if masked_ref is not None:
            masked_ref[block] = masked
        part = dot_nn(masked, rows_of(w_ref, block, ref.shape[1]))
        total = part if total is None else total + part
    return total.astype(BF16)


def context_grad_kernel(info, *refs):
    g_sources, parts, grad_ref, w_ref, wq_out = refs[:4], refs[4:14], *refs[14:17]
    g_ref, wq_ref, g_sems, w_sems, q_sems, out_sem = refs[17:]
    places = []
    q_copies = part_copies(info, parts, pl.ds(0, 3), wq_ref, q_sems, places)
    w_copies = part_copies(info, parts, 3, w_ref, w_sems)
    saves = []
    for copy, place in zip(q_copies, places):
        copy.wait()
        saves.append(
            pltpu.make_async_copy(wq_ref.at[:, place, :], wq_out.at[:, place, :], out_sem.at[len(saves)])
        )
        saves[-1].start()
    for copy in w_copies:
        copy.wait()

    @pl.when(info[4] == 1)
    def _():
        for copy in start_all(g_sources, g_ref, g_sems):
            copy.wait()
        grad_ref[...] = context_grad(info, [g_ref.at[i] for i in range(4)], w_ref)

    @pl.when(info[4] != 1)
    def _():
        grad_ref[...] = jnp.zeros_like(grad_ref)

    for copy in saves:
        copy.wait()


def attend_backward(qkv_ref, attend_ref, grad, gq_ref):
    scale = float(HEAD) ** -0.5
    for head, cols in enumerate(head_slices(grad.shape[1])):
        grad_head = grad[:, cols]
        queries, keys, values = (qkv_ref[c, :, cols] for c in range(3))
        attend = attend_ref[head]
        grad_attend = dot_nt(grad_head, values)
        gq_ref[2, :, cols] = dot_tn(attend.astype(BF16), grad_head).astype(BF16)
        inner = jnp.sum(grad_attend * attend, axis=-1, keepdims=True)
        grad_scores = (attend * (grad_attend - inner) * scale).astype(BF16)
        gq_ref[0, :, cols] = dot_nn(grad_scores, keys).astype(BF16)
        gq_ref[1, :, cols] = dot_tn(grad_scores, queries).astype(BF16)


def norm_parts(info, x_refs, mean, inverse, gq_ref, w_ref, stat_ref, norm_refs):
    width = x_refs[0].shape[1]
    plain, weighted = 0.0, 0.0
    by_rel = dict(zip(REL_GET, x_refs))
    out_by_rel = dict(zip(REL_PUT, norm_refs))
    for rel in REL_PUT:
        block = block_of(info, rel)
        part = None
        for c in range(3):
            term = dot_nt(gq_ref[c], rows_of(w_ref.at[c], block, width))
            part = term if part is None else part + term
        unit = (by_rel[rel][...].astype(F32) - mean) * inverse
        plain = plain + jnp.sum(part, axis=-1, keepdims=True)
        weighted = weighted + jnp.sum(part * unit, axis=-1, keepdims=True)
        ref = out_by_rel[rel]
        ref[:, :width] = part.astype(ref.dtype)
    stat_ref[:, 0:1] = plain
    stat_ref[:, 1:2] = weighted
    lane = lax.broadcasted_iota(jnp.int32, (plain.shape[0], 128), 1)
    plain_high, weighted_high = plain.astype(BF16).astype(F32), weighted.astype(BF16).astype(F32)
    packed = jnp.where(lane == 0, plain_high, jnp.where(lane == 1, plain - plain_high, 0.0))
    packed = jnp.where(lane == 2, weighted_high, jnp.where(lane == 3, weighted - weighted_high, packed))
    for ref in norm_refs[1:]:
        ref[:, width:] = packed.astype(BF16)


def middle_kernel(info, *refs):
    x_refs, grad_ref, w_ref = refs[:4], refs[4], refs[5]
    normed_ref, qkv_ref, attend_ref, context_ref, moment_ref, stat_ref = refs[6:12]
    norm_refs, gq_ref = refs[12:16], refs[16]
    mean, inverse = row_moments(x_refs)
    moment_ref[:, 0:1] = mean
    moment_ref[:, 1:2] = inverse
    queries, keys, values = project(info, x_refs, w_ref, mean, inverse, normed_ref)
    qkv_ref[0] = queries
    qkv_ref[1] = keys
    qkv_ref[2] = values
    for head, cols in enumerate(head_slices(queries.shape[1])):
        attend, context = attend_head(info, queries[:, cols], keys[:, cols], values[:, cols])
        attend_ref[head] = attend
        context_ref[:, cols] = context
    attend_backward(qkv_ref, attend_ref, grad_ref[...], gq_ref)
    norm_parts(info, x_refs, mean, inverse, gq_ref, w_ref, stat_ref, norm_refs)


def norm_kernel(info, *refs):
    x_refs, moment_ref, gq_ref, w_ref = refs[:4], refs[4], refs[5], refs[6]
    stat_ref, norm_refs = refs[7], refs[8:12]
    mean, inverse = moment_ref[:, 0:1], moment_ref[:, 1:2]
    norm_parts(info, x_refs, mean, inverse, gq_ref, w_ref, stat_ref, norm_refs)


def last_kernel(info, *refs):
    g_refs, w_ref, qkv_ref, attend_ref, normed_ref, context_ref = refs[:4], *refs[4:9]
    gq_ref, outs = refs[9], refs[10:18]
    masked_ref, block_ref = refs[18:20]
    grad = context_grad(info, g_refs, w_ref, masked_ref)
    attend_backward(qkv_ref, attend_ref, grad, gq_ref)
    rows = outs[0].shape[-2]
    for c in range(4):
        for z in range(4):
            left = normed_ref[z] if c < 3 else masked_ref[z]
            right = gq_ref[c] if c < 3 else context_ref[...]
            block_ref[c, pl.ds(z * left.shape[1], left.shape[1]), :] = dot_tn(left, right).astype(BF16)
    for side in range(2):
        core = info[3] if side == 0 else 1 - info[3]
        for far, rel_far in enumerate(REL_PUT):
            for near, rel_near in enumerate(REL_PUT):
                place = pl.ds(place_row(info, rel_near, rel_far, core, rows), rows)
                for c in range(4):
                    outs[side * 4 + far][near, c] = block_ref[c, place, :]


VMEM = pl.BlockSpec(memory_space=pltpu.VMEM)
SMEM = pl.BlockSpec(memory_space=pltpu.SMEM)
ANY = pl.BlockSpec(memory_space=pl.ANY)


def call(kernel, outs, in_specs, scratch, flops, args, megabytes, out_specs=None):
    moved = sum(a.size * a.dtype.itemsize for a in args)
    return pl.pallas_call(
        kernel,
        out_shape=outs,
        in_specs=in_specs,
        out_specs=out_specs or [VMEM] * len(outs),
        scratch_shapes=scratch,
        compiler_params=pltpu.CompilerParams(vmem_limit_bytes=megabytes << 20),
        cost_estimate=pl.CostEstimate(flops=flops, bytes_accessed=moved, transcendentals=0),
    )(*args)


def shape(dims, dtype=BF16):
    return jax.ShapeDtypeStruct(dims, dtype)


def local(frames, lengths, qkv_weight, out_weight, grad_out):
    rows, own_width = frames.shape
    shard_rows, heads_width = qkv_weight.shape[2:]
    heads = heads_width // HEAD
    width = own_width * lax.axis_size("tensor")
    place = lax.axis_index("fsdp")
    section = lax.axis_index("section")
    on_first = section == 0
    info = jnp.stack(
        [lax.axis_index("tensor"), place // 8, place // 2 % 4, place % 2, section, lengths[0]]
    ).astype(jnp.int32)
    live_rows = (jnp.arange(rows, dtype=jnp.int32)[:, None] < lengths[0]).astype(F32)

    shard = jnp.concatenate([qkv_weight[0], out_weight[0].T[None]], 0)
    w_parts, x_first, g_first, ready = gather_weights(shard, frames, grad_out)

    block = (rows, own_width)
    wide = (rows, own_width + 128)
    wq_dims, wo_dims = (3, width, heads_width), (width, heads_width)
    project_flops = 2 * rows * width * 3 * heads_width
    part_sems = pltpu.SemaphoreType.DMA((32,))
    piece_sems = pltpu.SemaphoreType.DMA((4,))
    mixed = call(
        first_kernel,
        [shape(block, F32), shape(block), shape(block), shape(block)],
        [SMEM] + [ANY] * 15,
        [
            pltpu.VMEM((4, *block), BF16),
            pltpu.VMEM(wq_dims, BF16),
            pltpu.VMEM(wo_dims, BF16),
            pltpu.VMEM((rows, heads_width), BF16),
            piece_sems,
            part_sems,
            part_sems,
        ],
        4 * project_flops // 3,
        (info, *x_first, *w_parts, ready),
        56,
    )

    def finish(x_own, moments, stats, parts, own_grad):
        opposite = shift_tensor(parts[3], 2)
        arrived = [shift_tensor(parts[1], 1), shift_tensor(parts[2], -1), opposite]
        norm_grad = parts[0]
        plain, weighted = stats[:, 0:1], stats[:, 1:2]
        for part in arrived:
            part = part.astype(F32)
            norm_grad = norm_grad + part[:, :own_width]
            sums = part[:, own_width : own_width + 4]
            plain = plain + (sums[:, 0:1] + sums[:, 1:2])
            weighted = weighted + (sums[:, 2:3] + sums[:, 3:4])
        mean, inverse = moments[:, 0:1], moments[:, 1:2]
        unit = (x_own.astype(F32) - mean) * inverse
        centered = norm_grad - plain / width - unit * (weighted / width)
        return (own_grad.astype(F32) + inverse * centered).astype(BF16)

    opposite = shift_tensor(mixed[3], 2)
    arrived = [shift_tensor(mixed[1], 1), shift_tensor(mixed[2], -1), opposite]
    mixed_own = mixed[0] + sum(part.astype(F32) for part in arrived)
    first_out = (frames.astype(F32) + live_rows * mixed_own).astype(BF16)
    grad_top, w_out, w_qkv = call(
        context_grad_kernel,
        [shape((rows, heads_width)), shape(wo_dims), shape(wq_dims)],
        [SMEM] + [ANY] * 14,
        [
            pltpu.VMEM((4, *block), BF16),
            pltpu.VMEM(wq_dims, BF16),
            piece_sems,
            part_sems,
            part_sems,
            part_sems,
        ],
        project_flops // 3,
        (info, *g_first, *w_parts),
        56,
        [VMEM, VMEM, ANY],
    )
    first_out, grad_top = lax.optimization_barrier((first_out, grad_top))

    entry = jnp.where(on_first, frames, cross_section(first_out, 0))
    x_entry = gather_tensor(entry)
    (w_loaded,) = call(
        load_kernel,
        [shape(wq_dims)],
        [ANY],
        [pltpu.SemaphoreType.DMA(())],
        0,
        (lax.optimization_barrier((w_qkv, entry))[0],),
        8,
    )
    norm_outs = [shape((rows, 2), F32), shape(block, F32), shape(wide), shape(wide), shape(wide)]
    normed, qkv, attend, context, moments, stats, *parts = call(
        middle_kernel,
        [
            shape((4, *block)),
            shape((3, rows, heads_width)),
            shape((heads, rows, rows), F32),
            shape((rows, heads_width)),
            shape((rows, 2), F32),
        ]
        + norm_outs,
        [SMEM] + [VMEM] * 6,
        [pltpu.VMEM((3, rows, heads_width), BF16)],
        2 * project_flops,
        (info, *x_entry, grad_top, w_loaded),
        16,
    )
    upper_grad = finish(x_entry[0], moments, stats, parts, grad_out)
    top_grad = jnp.where(on_first, cross_section(upper_grad, 1), grad_out)
    gq, *blocks = call(
        last_kernel,
        [shape((3, rows, heads_width))] + [shape((4, 4, shard_rows, heads_width))] * 8,
        [SMEM] + [VMEM] * 9,
        [pltpu.VMEM((4, *block), BF16), pltpu.VMEM((4, *wo_dims), BF16)],
        2 * project_flops,
        (info, *gather_tensor(top_grad), w_out, qkv, attend, normed, context),
        28,
    )
    arrived = {i: swap_cores(blocks[4 + i]) for i in (3, 1, 2, 0)}
    gq, arrived[3] = lax.optimization_barrier((gq, arrived[3]))
    line = add(*ring_put([add(blocks[i], arrived[i]) for i in range(4)], FAR))
    terms = ring_put([line[i] for i in range(4)], NEAR)
    qkv_grad = add(*(term[:3] for term in terms))
    out_grad = add(*(term[3] for term in terms)).T
    stats, *parts = call(
        norm_kernel,
        norm_outs,
        [SMEM] + [VMEM] * 7,
        [],
        project_flops,
        (info, *x_entry, moments, gq, w_qkv),
        16,
    )
    grad_in = finish(x_entry[0], moments, stats, parts, top_grad)
    return (grad_in[None], qkv_grad[None], out_grad[None])


def solution(mesh):
    in_specs = (
        P("fsdp", "tensor"),
        P("fsdp"),
        P("section", None, "fsdp", "tensor"),
        P("section", "tensor", "fsdp"),
        P("fsdp", "tensor"),
    )
    out_specs = (
        P("section", "fsdp", "tensor"),
        P("section", None, "fsdp", "tensor"),
        P("section", "tensor", "fsdp"),
    )
    return jax.shard_map(local, mesh=mesh, in_specs=in_specs, out_specs=out_specs, check_vma=False)
```
